32 devices in a mesh: groups: 2 (over y), seq: 4 (over z), head: 2 (over x), prompt: 2 (over core).
Axes of the slice: x: 2, y: 2, z: 4, core: 2. Of those that a mesh axis runs over, the one named last changes fastest.
Arguments:
- prompt_queries: bfloat16 [4, 512, 2048], P(('groups', 'prompt'), 'seq', 'head'), parts along dimension 0, may hold values from -6 to 6
- prompt_keys: bfloat16 [4, 512, 2048], P(('groups', 'prompt'), 'seq', 'head'), parts along dimension 0, may hold values from -20 to 20
- prompt_values: bfloat16 [4, 512, 4096], P(('groups', 'prompt'), 'seq', 'head'), parts along dimension 0, may hold values from -6 to 6
- prompt_beta: float32 [4, 32, 512], P(('groups', 'prompt'), 'head', 'seq'), parts along dimension 0, may hold values from 0.005 to 0.15
- prompt_decay: float32 [4, 32, 512], P(('groups', 'prompt'), 'head', 'seq'), parts along dimension 0, may hold values from -0.7 to 0
- suffix_queries: bfloat16 [32, 256, 2048], P(('groups', 'seq', 'prompt'), None, 'head'), parts along dimension 0, may hold values from -6 to 6
- suffix_keys: bfloat16 [32, 256, 2048], P(('groups', 'seq', 'prompt'), None, 'head'), parts along dimension 0, may hold values from -20 to 20
- suffix_values: bfloat16 [32, 256, 4096], P(('groups', 'seq', 'prompt'), None, 'head'), parts along dimension 0, may hold values from -6 to 6
- suffix_beta: float32 [32, 32, 256], P(('groups', 'seq', 'prompt'), 'head'), parts along dimension 0, may hold values from 0.005 to 0.15
- suffix_decay: float32 [32, 32, 256], P(('groups', 'seq', 'prompt'), 'head'), parts along dimension 0, may hold values from -0.2 to 0
- norm_gain: float32 [128], replicated, may hold values from 0.25 to 1.75
- slot_branch: int32 [32], P('groups'), parts along dimension 0, may hold values from 0 to 15, each once
- branch_length: int32 [32], P('groups'), parts along dimension 0, may hold values from 1 to 256, 2048 in all
- branch_prompt: int32 [32], P('groups'), parts along dimension 0, may hold values from 0 to 1
Outputs:
- prompt_out: bfloat16 [4, 512, 4096], P(('groups', 'prompt'), 'seq', 'head'), parts along dimension 0
- suffix_out: bfloat16 [32, 256, 4096], P(('groups', 'seq', 'prompt'), None, 'head'), parts along dimension 0
The draws below stay inside these ranges and needn't reach their ends.
There are 2 independent parts, one for each index of `groups`. The reference program is written for one: setup_inputs(seed, part) draws one part's arguments, and reference() takes and returns one part's arrays. A program takes and returns all parts, laid end to end along the dimension named above; an argument that names none is the same for every part. Nothing has to cross between parts.
Inputs may be any that keep to these rules, and one draw needn't show every extreme that they name: slot_branch names every branch exactly once. `branch_length`: the lengths sum to 2048 and one of them is exactly 256.
All inputs are finite; a program needn't handle non-finite values.
Results may differ from the reference program's by a relative error of at most 0.0067.
Values sent between devices are 32-bit elements; how exact they have to be, the bound alone decides.
A program may use at most 128 MiB of HBM per device.

```python
import math
import jax
import jax.numpy as jnp
import numpy as np
from jax import lax

DK = 128
DV = 128
OUTPUT_HEAD_NUM = 32
HK = 16
TOK_DEV = 128
SUF = 256
QUERY_TEXT_SPAN = 512
PROMPT_COUNT = 2
BRANCHES = 16


def fast_heads(key):
    head_picks = jax.random.randint(jax.random.fold_in(key, 101), (OUTPUT_HEAD_NUM,), 0, 2)
    return head_picks == 0


def channel_scales(key):
    return jnp.exp(jax.random.uniform(jax.random.fold_in(key, 202), (HK * DK,), jnp.float32, -1.2, 1.2))


def key_draw(key, noise_generator_key, shape):
    noise_part = jnp.clip(jax.random.normal(jax.random.fold_in(key, noise_generator_key), shape, jnp.float32), -4.0, 4.0)
    return (noise_part * channel_scales(key)).astype(jnp.bfloat16)


def beta_draw(key, noise_generator_key, prefix_number, length):
    quick_channel_selector = fast_heads(key)[None, :, None]
    quick_forget_bound = jax.random.uniform(jax.random.fold_in(key, noise_generator_key), (prefix_number, OUTPUT_HEAD_NUM, 1), jnp.float32, 0.02, 0.1)
    gentle = jnp.exp(jax.random.uniform(jax.random.fold_in(key, noise_generator_key + 1), (prefix_number, OUTPUT_HEAD_NUM, 1), jnp.float32, -4.6, -3.0))
    jitter = jax.random.uniform(jax.random.fold_in(key, noise_generator_key + 2), (prefix_number, OUTPUT_HEAD_NUM, length), jnp.float32, 0.6, 1.4)
    return jnp.where(quick_channel_selector, quick_forget_bound, gentle) * jitter


def decay_draw(key, noise_generator_key, prefix_number, length, tile_extent):
    quick_channel_selector = fast_heads(key)[None, :, None]
    tile_total = length // tile_extent
    spike_span = min(32, tile_extent // 4)
    quick_forget_bound = jax.random.uniform(jax.random.fold_in(key, noise_generator_key), (prefix_number, OUTPUT_HEAD_NUM, 1), jnp.float32, 1.0 / 50.0, 1.0 / 40.0)
    spike_start_slot = jax.random.randint(jax.random.fold_in(key, noise_generator_key + 3), (prefix_number, OUTPUT_HEAD_NUM, tile_total), 0, tile_extent - spike_span + 1)
    spike_start_slot = jnp.repeat(spike_start_slot, tile_extent, axis=2)
    tile_offset = (jnp.arange(length, dtype=jnp.int32) % tile_extent)[None, None, :]
    within_spike = (tile_offset >= spike_start_slot) & (tile_offset < spike_start_slot + spike_span)
    forget_lower_bound = jnp.where(quick_channel_selector & within_spike, quick_forget_bound, 0.25 / QUERY_TEXT_SPAN)
    spread_factor = jnp.exp(jax.random.uniform(jax.random.fold_in(key, noise_generator_key + 1), (prefix_number, OUTPUT_HEAD_NUM, tile_total), jnp.float32, -0.7, 0.7))
    spread_factor = jnp.repeat(spread_factor, tile_extent, axis=2)
    jitter = jax.random.uniform(jax.random.fold_in(key, noise_generator_key + 2), (prefix_number, OUTPUT_HEAD_NUM, length), jnp.float32, 0.7, 1.3)
    return -forget_lower_bound * spread_factor * jitter


def draw_prompt_keys(key, part):
    return key_draw(key, 211, (PROMPT_COUNT, QUERY_TEXT_SPAN, HK * DK))


def draw_suffix_keys(key, part):
    return key_draw(key, 221, (BRANCHES, SUF, HK * DK))


def draw_prompt_beta(key, part):
    return beta_draw(key, 411, PROMPT_COUNT, QUERY_TEXT_SPAN)


def draw_suffix_beta(key, part):
    return beta_draw(key, 421, BRANCHES, SUF)


def draw_prompt_decay(key, part):
    smoothed_decay = decay_draw(key, 311, PROMPT_COUNT, QUERY_TEXT_SPAN, TOK_DEV)
    spike_positions = jax.random.randint(jax.random.fold_in(key, 321), (PROMPT_COUNT, OUTPUT_HEAD_NUM, 3), 0, QUERY_TEXT_SPAN)
    place_indices = jnp.arange(QUERY_TEXT_SPAN, dtype=jnp.int32)
    spike_events = jnp.any(place_indices[None, None, :, None] == spike_positions[:, :, None, :], axis=-1)
    spike_decays = jnp.log(jax.random.uniform(jax.random.fold_in(key, 322), (PROMPT_COUNT, OUTPUT_HEAD_NUM, QUERY_TEXT_SPAN), jnp.float32, 0.5, 0.8))
    return jnp.where(spike_events, spike_decays, smoothed_decay)


def draw_suffix_decay(key, part):
    return decay_draw(key, 331, BRANCHES, SUF, SUF)


def with_ends(values, own_key, least, largest):
    index_at = [jax.random.randint(jax.random.fold_in(own_key, axis), (), 0, length) for axis, length in enumerate(values.shape)]
    main_axis = values.shape.index(max(values.shape))
    neighbour = index_at[:main_axis] + [(index_at[main_axis] + 1) % values.shape[main_axis]] + index_at[main_axis + 1:]
    return values.at[tuple(index_at)].set(least).at[tuple(neighbour)].set(largest)


def level_of(stream_key, dims, shards, smallest, top_value):
    gain, own = 1.0, jax.random.fold_in(stream_key, 6)
    for dim, shards_of in shards:
        heights = jnp.exp(jax.random.uniform(jax.random.fold_in(own, dim), (shards_of,), jnp.float32, smallest / len(shards), top_value / len(shards)))
        gain = gain * jnp.repeat(heights, dims[dim] // shards_of).reshape([-1 if axis == dim else 1 for axis in range(len(dims))])
    return gain


def length_profile(count, total, bound, slope):
    weights = [(1 << 20) // math.isqrt(grade ** slope) + 1 for grade in range(2, count + 1)]
    rest, holding = total - bound - (count - 1), [1] * (count - 1)
    while rest > 0:
        candidates = [i for i in range(count - 1) if holding[i] < bound]
        whole, left = sum([weights[i] for i in candidates]), rest
        for i in candidates:
            extra = min(bound - holding[i], max(1, left * weights[i] // whole), rest)
            holding[i] = holding[i] + extra
            rest = rest - extra
    return np.array([bound] + holding)


def ragged_sizes(key, number_of, total, most, skew):
    if number_of == 2:
        one = jax.random.randint(key, (), max(1, total - most), min(most, total - 1) + 1)
        return jnp.stack([one, total - one])
    sizes = jnp.asarray(length_profile(number_of, total, most, skew), jnp.int32)
    pairs = (number_of - 1) // 2
    source_of, receiver = sizes[1:1 + 2 * pairs:2], sizes[2:2 + 2 * pairs:2]
    margin = jnp.minimum(source_of - 1, most - receiver)
    shifted = jax.random.randint(jax.random.fold_in(key, 1), (pairs,), 0, 1 << 20) % (margin + 1)
    sizes = sizes.at[1:1 + 2 * pairs:2].set(source_of - shifted).at[2:2 + 2 * pairs:2].set(receiver + shifted)
    return sizes[jax.random.permutation(jax.random.fold_in(key, 2), number_of)]


def centred(own_key, extent, width, most, cuts=(), kind=jnp.bfloat16):
    entries = width * jax.random.normal(own_key, extent, jnp.float32)
    if cuts:
        entries = entries * level_of(own_key, extent, cuts, -0.22, 0.18)
    return jnp.clip(entries, -most, most).astype(kind)


def setup_inputs(seed: int = 0, part: int = 0) -> dict:
    streams_of = jax.random.split(jax.random.key(seed), 15)
    own_keys = jax.random.split(jax.random.fold_in(streams_of[14], part), 15)
    prompt_queries = centred(own_keys[0], (PROMPT_COUNT, QUERY_TEXT_SPAN, HK * DK), 1.0, 6.0, ((0, 2), (1, 4), (2, 2)))
    prompt_keys = draw_prompt_keys(jax.random.fold_in(jax.random.fold_in(streams_of[14], part), 71), part)
    prompt_values = centred(own_keys[2], (PROMPT_COUNT, QUERY_TEXT_SPAN, OUTPUT_HEAD_NUM * DV), 1.0, 6.0, ((0, 2), (1, 4), (2, 2)))
    prompt_beta = draw_prompt_beta(jax.random.fold_in(jax.random.fold_in(streams_of[14], part), 71), part)
    prompt_decay = draw_prompt_decay(jax.random.fold_in(jax.random.fold_in(streams_of[14], part), 71), part)
    suffix_queries = centred(own_keys[5], (BRANCHES, SUF, HK * DK), 1.0, 6.0, ((0, 8), (2, 2)))
    suffix_keys = draw_suffix_keys(jax.random.fold_in(jax.random.fold_in(streams_of[14], part), 71), part)
    suffix_values = centred(own_keys[7], (BRANCHES, SUF, OUTPUT_HEAD_NUM * DV), 1.0, 6.0, ((0, 8), (2, 2)))
    suffix_beta = draw_suffix_beta(jax.random.fold_in(jax.random.fold_in(streams_of[14], part), 71), part)
    suffix_decay = draw_suffix_decay(jax.random.fold_in(jax.random.fold_in(streams_of[14], part), 71), part)
    norm_gain = jnp.clip(1.0 + 0.15 * jax.random.normal(streams_of[10], (DV,), jnp.float32), 0.25, 1.75)
    slot_branch = jax.random.permutation(own_keys[11], BRANCHES).astype(jnp.int32)
    branch_length = ragged_sizes(own_keys[12], BRANCHES, BRANCHES * SUF // 2, SUF, 2).astype(jnp.int32)
    branch_prompt = with_ends(jax.random.randint(own_keys[13], (BRANCHES,), 0, PROMPT_COUNT), jax.random.fold_in(own_keys[13], 1), 0, PROMPT_COUNT - 1).astype(jnp.int32)
    return {"prompt_queries": prompt_queries, "prompt_keys": prompt_keys, "prompt_values": prompt_values, "prompt_beta": prompt_beta, "prompt_decay": prompt_decay, "suffix_queries": suffix_queries, "suffix_keys": suffix_keys, "suffix_values": suffix_values, "suffix_beta": suffix_beta, "suffix_decay": suffix_decay, "norm_gain": norm_gain, "slot_branch": slot_branch, "branch_length": branch_length, "branch_prompt": branch_prompt}


HIGH_PRECISION = lax.Precision.HIGHEST
EPS_NORM = 1e-06

def unit_rows(vectors):
    widened = vectors.astype(jnp.float32)
    factor = lax.rsqrt(lax.optimization_barrier(jnp.sum(widened * widened, axis=-1, keepdims=True)) + EPS_NORM)
    return (widened * factor).astype(jnp.bfloat16)

def normed(raw_out, norm_gain):
    inv_rms = lax.rsqrt(lax.optimization_barrier(jnp.mean(raw_out * raw_out, axis=-1, keepdims=True)) + EPS_NORM)
    return (raw_out * inv_rms * norm_gain).astype(jnp.bfloat16)

def prepare(queries, key_rows, value_rows, beta_rows, decay_rows):
    tokens = queries.shape[0]
    query_unit = jnp.repeat(unit_rows(queries.reshape(tokens, HK, DK)), OUTPUT_HEAD_NUM // HK, axis=1)
    key_unit = jnp.repeat(unit_rows(key_rows.reshape(tokens, HK, DK)), OUTPUT_HEAD_NUM // HK, axis=1)
    return (query_unit, key_unit, value_rows.reshape(tokens, OUTPUT_HEAD_NUM, DV), beta_rows.T, decay_rows.T)

def run_chain(start_state, query_unit, key_unit, value_rows, beta_rows, decay_rows):

    def advance(present_state, inputs):
        query_current, key_now, value_now, beta_now, decay_now = inputs
        key_single = key_now.astype(jnp.float32)
        faded_state = jnp.exp(decay_now)[:, None, None] * present_state
        retrieved_value = jnp.einsum('te,tei->ti', key_single, faded_state, precision=HIGH_PRECISION)
        written = beta_now[:, None] * (value_now.astype(jnp.float32) - retrieved_value)
        present_state = faded_state + key_single[:, :, None] * written[:, None, :]
        output_rows = jnp.einsum('te,tei->ti', query_current.astype(jnp.float32), present_state, precision=HIGH_PRECISION)
        return (present_state, output_rows)
    return lax.scan(advance, start_state, (query_unit, key_unit, value_rows, beta_rows, decay_rows))

def reference(prompt_queries, prompt_keys, prompt_values, prompt_beta, prompt_decay, suffix_queries, suffix_keys, suffix_values, suffix_beta, suffix_decay, norm_gain, slot_branch, branch_length, branch_prompt):
    zero_state = jnp.zeros((OUTPUT_HEAD_NUM, DK, DV), jnp.float32)
    finals = []
    prompt_rows = []
    for prompt_index in range(PROMPT_COUNT):
        prepared = prepare(prompt_queries[prompt_index], prompt_keys[prompt_index], prompt_values[prompt_index], prompt_beta[prompt_index], prompt_decay[prompt_index])
        final_state, output_rows = run_chain(zero_state, prepared[0], prepared[1], prepared[2], prepared[3], prepared[4])
        finals.append(final_state)
        prompt_rows.append(normed(output_rows, norm_gain).reshape(QUERY_TEXT_SPAN, OUTPUT_HEAD_NUM * DV))
    prompt_out = jnp.stack(prompt_rows)
    final_states = jnp.stack(finals)
    slot_index = slot_branch.astype(jnp.int32)
    lengths = branch_length[slot_index]
    owners = branch_prompt[slot_index].astype(jnp.int32)
    seed_states = final_states[owners]

    def run_slot(seed_state, queries, key_rows, value_rows, beta_rows, decay_rows):
        prepared = prepare(queries, key_rows, value_rows, beta_rows, decay_rows)
        ignored, output_rows = run_chain(seed_state, prepared[0], prepared[1], prepared[2], prepared[3], prepared[4])
        return normed(output_rows, norm_gain)
    suffix_rows = jax.vmap(run_slot)(seed_states, suffix_queries, suffix_keys, suffix_values, suffix_beta, suffix_decay)
    live_rows = jnp.arange(SUF, dtype=jnp.int32)[None, :] < lengths[:, None]
    suffix_out = jnp.where(live_rows[:, :, None, None], suffix_rows, jnp.zeros((), jnp.bfloat16)).reshape(BRANCHES, SUF, OUTPUT_HEAD_NUM * DV)
    return (prompt_out, suffix_out)
```

```python
import functools

import jax
import jax.numpy as jnp
import ml_dtypes
import numpy as np
from jax import lax
from jax.experimental import pallas as pl
from jax.experimental.pallas import tpu as pltpu
from jax.sharding import PartitionSpec as P

DK = 128
DV = 128
CH = 128
SB = 16
REP = 2
EPS_NORM = 1e-06
F32 = jnp.float32
BF16 = jnp.bfloat16
MESH = pl.DeviceIdType.MESH
NN = (((1,), (0,)), ((), ()))
NT = (((1,), (1,)), ((), ()))
TN = (((0,), (0,)), ((), ()))

BD = {16: 0, 32: 2, 64: 4}
SWAP = {16: 1, 32: 3, 64: 5}
UPTO, BACKWARDS, THIN = 6, 7, 8
EVEN = {16: 0, 32: 32, 64: 64}
ODD = {16: 16, 32: 48, 64: 80}
STRICT, EYE = 96, 112


def tables():
    l = np.arange(CH)
    r, c = l[:, None], l[None]
    i = np.arange(SB)[:, None]
    squares = []
    for s in (16, 32, 64):
        squares += [r // s == c // s, (r // s) ^ 1 == c // s]
    thin = []
    for s in (16, 32, 64):
        thin += [np.broadcast_to((c // s) % 2 == p, (SB, CH)) for p in (0, 1)]
    thin += [i > c % SB, i == c % SB]
    squares += [r >= c, r ^ (CH - SB) == c, np.concatenate(thin, 0)]
    cum = np.concatenate([r <= c, r <= (c ^ (CH - SB))], 1)
    pick = np.concatenate([r == (c // SB) * SB + k for k in range(SB)], 1)
    b = lambda x: x.astype(np.float32).astype(ml_dtypes.bfloat16)
    return b(np.stack(squares)), b(cum), b(pick)


def mm(a, b, dims=NN):
    return lax.dot_general(a, b, dims, preferred_element_type=F32)


def unit(x):
    w = x.astype(F32)
    return (w * lax.rsqrt(jnp.sum(w * w, axis=-1, keepdims=True) + EPS_NORM)).astype(BF16)


def flip(x):
    return jnp.concatenate([x[i : i + SB] for i in range(CH - SB, -1, -SB)], axis=0)


def tile(x, n):
    return x if n == 1 else jnp.concatenate([x] * n, axis=0)


def terms(x, n):
    parts = []
    for _ in range(n):
        p = x.astype(BF16)
        parts.append(p)
        x = x - p.astype(F32)
    return jnp.concatenate(parts, axis=1)


def running_log(decay, cum):
    both = mm(terms(decay, 3), tile(cum[...], 3))
    return both[:, :CH], both[:, CH:]


def spread_beta(beta, masks):
    eye = masks[THIN, EYE:].astype(F32)
    rows = jnp.concatenate([beta[h : h + 1] * eye for h in range(beta.shape[0])], axis=0)
    return mm(terms(rows, 2), tile(masks[BD[16]], 2))


def inverses(grams, betas, masks, pick):
    n = len(grams)
    blocks = CH // SB
    thin = lambda at: masks[THIN, at : at + SB]
    strict = thin(STRICT)
    compact = []
    for g in grams:
        c = g[:SB, :CH] * masks[BD[16], :SB]
        for b in range(1, blocks):
            c = c + g[b * SB : (b + 1) * SB, :CH] * masks[BD[16], b * SB : (b + 1) * SB]
        compact.append(c * strict)
    flat = jnp.concatenate(compact, axis=0)
    eye = thin(EYE).astype(F32)
    top = [-eye[:8]] * (n * REP)
    low = [-eye[8:]] * (n * REP)
    for k in range(SB - 1):
        if k % 2 == 0:
            pair = mm(flat, pick[:, k * CH : (k + 2) * CH])
        e = pair[:, (k % 2) * CH : (k % 2 + 1) * CH]
        for j in range(n):
            for r in range(REP):
                h = j * REP + r
                row = (top[h][k : k + 1] if k < 8 else low[h][k - 8 : k - 7]) * betas[h][k : k + 1]
                if k < 7:
                    top[h] = top[h] - e[j * SB : j * SB + 8] * row
                low[h] = low[h] - e[j * SB + 8 : (j + 1) * SB] * row
    done = [
        (jnp.concatenate([top[h], low[h]], axis=0) * betas[h]).astype(BF16) for h in range(n * REP)
    ]
    first = done[0::2]
    second = mm(jnp.concatenate(done[1::2], axis=0), masks[BACKWARDS]).astype(BF16)
    second = [second[j * SB : (j + 1) * SB] for j in range(n)]
    size = SB
    while size < CH:
        rows = size // SB
        even, odd = tile(thin(EVEN[size]), rows), tile(thin(ODD[size]), rows)
        cross = []
        for g in grams:
            parts = []
            for i in range(rows):
                part = None
                for p in range(CH // (2 * size)):
                    at = (2 * p + 1) * size + i * SB
                    ahead = masks[BD[size], 2 * p * size : 2 * p * size + SB]
                    behind = masks[BD[size], (2 * p + 1) * size : (2 * p + 1) * size + SB]
                    back = CH - SB - (2 * p * size + i * SB)
                    term = g[at : at + SB, :CH] * ahead + g[back : back + SB, CH:] * behind
                    part = term if part is None else part + term
                parts.append(part)
            cross.append(jnp.concatenate(parts, axis=0))
        reps = CH // size
        split = [(a * even, a * odd, b * even, b * odd) for a, b in zip(first, second)]
        mids = [
            mm(c, tile(ae + bo, reps) * masks[BD[size]]).astype(BF16)
            for c, (ae, ao, be, bo) in zip(cross, split)
        ]
        offs = [
            mm(ao + be, tile(m, reps) * masks[SWAP[size]]).astype(BF16)
            for m, (ae, ao, be, bo) in zip(mids, split)
        ]
        first = [
            jnp.concatenate([ae, o * even + ao], axis=0) for o, (ae, ao, be, bo) in zip(offs, split)
        ]
        second = [
            jnp.concatenate([be + o * odd, bo], axis=0) for o, (ae, ao, be, bo) in zip(offs, split)
        ]
        size *= 2
    return first, [flip(x) for x in second]


def solve(queries, keys, betas, masks, pick):
    qs, ks = [unit(q) for q in queries], [unit(k) for k in keys]
    backs = [flip(k) for k in ks]
    looks = [mm(q, k, NT).astype(BF16) * masks[UPTO] for q, k in zip(qs, ks)]
    grams = [mm(k, jnp.concatenate([k, b], axis=0), NT).astype(BF16) for k, b in zip(ks, backs)]
    return qs, ks, backs, looks, inverses(grams, betas, masks, pick)


def norm_rows(o, gain):
    return o * lax.rsqrt(jnp.mean(o * o, axis=-1, keepdims=True) + EPS_NORM) * gain


def chain_kernel(
    *refs,
):
    count = len(LOADED)
    given, facts, outs = refs[:count], refs[count : count + 3], refs[count + 3 : count + 5]
    held, rest = refs[count + 5 : 2 * count + 5], refs[2 * count + 5 :]
    pq, pk, pv, pbeta, pdecay, sq, sk, sv, sbeta, sdecay, gain_ref, masks, cum, pick = held
    slot_branch, branch_length, branch_prompt = facts
    (
        pout, sout, step_ref, seen_ref, fade_ref, inbox, outbox, finals,
        s_left, s_look, s_key, s_eps, s_end, x_step, x_near_step, x_near_base, x_near_fade,
        load_sem, pout_sem, sout_sem,
        fsend, frecv, bsend, brecv, csend, crecv, xsend, xrecv,
    ) = rest
    key_heads = pq.shape[2] // DK
    heads = key_heads * REP
    slots, spans = sq.shape[0], sq.shape[1] // CH
    pack = PACK if key_heads % PACK == 0 else key_heads
    packs = key_heads // pack
    rank, last = lax.axis_index("seq"), lax.axis_size("seq") - 1
    mine = lax.axis_index("prompt")
    other = 1 - mine
    short = x_step.shape[0]
    first_short = heads - short

    def load(name):
        n = LOADED.index(name)
        return pltpu.make_async_copy(given[n], held[n], load_sem.at[n])

    for name in LOAD_ORDER:
        load(name).start()

    def save_prompt(h):
        at = (0, slice(None), pl.ds(pl.multiple_of(h * DV, DV), DV))
        return pltpu.make_async_copy(pout.at[at], outs[0].at[at], pout_sem.at[h])

    def save_slot(j):
        at = (slice(None), slice(None), pl.ds(pl.multiple_of(j * REP * DV, REP * DV), REP * DV))
        return pltpu.make_async_copy(sout.at[at], outs[1].at[at], sout_sem.at[j])

    def lend(n, part):
        src = (x_step.at[n], outbox.at[first_short + n], fade_ref.at[first_short + n])[part]
        dst = (x_near_step.at[n], x_near_base.at[n], x_near_fade.at[n])[part]
        return pltpu.make_async_remote_copy(
            src_ref=src, dst_ref=dst, send_sem=xsend.at[n, part], recv_sem=xrecv.at[n, part],
            device_id={"seq": rank - 1}, device_id_type=MESH,
        )

    def forward(i):
        return pltpu.make_async_remote_copy(
            src_ref=outbox.at[i], dst_ref=inbox.at[i], send_sem=fsend.at[i],
            recv_sem=frecv.at[i], device_id={"seq": rank + 1}, device_id_type=MESH,
        )

    def backward(i):
        return pltpu.make_async_remote_copy(
            src_ref=finals.at[mine, i], dst_ref=finals.at[mine, i], send_sem=bsend.at[i],
            recv_sem=brecv.at[i], device_id={"seq": rank - 1}, device_id_type=MESH,
        )

    def across(p, i):
        return pltpu.make_async_remote_copy(
            src_ref=finals.at[p, i], dst_ref=finals.at[p, i], send_sem=csend.at[i],
            recv_sem=crecv.at[i], device_id={"prompt": other}, device_id_type=MESH,
        )

    barrier = pltpu.get_barrier_semaphore()

    def greet(where):
        pl.semaphore_signal(barrier, inc=1, device_id=where, device_id_type=MESH)

    greet({"prompt": other})

    @pl.when(rank > 0)
    def _():
        greet({"seq": rank - 1})

    @pl.when(rank < last)
    def _():
        greet({"seq": rank + 1})

    def meet():
        pl.semaphore_wait(barrier, 1 + jnp.where(rank > 0, 1, 0) + jnp.where(rank < last, 1, 0))

    for name in FIRST_LOADS:
        load(name).wait()

    def prepare(g):
        span = slice(g * pack, (g + 1) * pack)
        cols = [slice(j * DK, (j + 1) * DK) for j in range(g * pack, (g + 1) * pack)]
        hs = slice(g * pack * REP, (g + 1) * pack * REP)
        log_row, log_back = running_log(pdecay[0, hs], cum)
        beta = spread_beta(pbeta[0, hs], masks)
        betas = [beta[h * SB : (h + 1) * SB] for h in range(pack * REP)]
        mid = log_row[:, CH // 2 - 1 : CH // 2]
        end = log_row[:, CH - 1 :]
        grow = (-jnp.exp(mid - log_row), -jnp.exp(mid - log_back))
        shrink = jnp.exp(log_row - mid).T
        at_mid, at_end, from_mid = jnp.exp(mid), jnp.exp(end), jnp.exp(end - mid)
        qs, ks, backs, looks, (first, second) = solve(
            [pq[0, :, c] for c in cols], [pk[0, :, c] for c in cols], betas, masks, pick
        )
        for j in range(pack):
            right = []
            for r, left in enumerate((first[j], second[j])):
                h = j * REP + r
                v = pv[0, :, (hs.start + h) * DV : (hs.start + h + 1) * DV]
                k, v = (ks[j], v) if r == 0 else (backs[j], flip(v))
                scaled = (left.astype(F32) * grow[r][h : h + 1]).astype(BF16)
                right += [mm(left, k).astype(BF16), mm(scaled, v).astype(BF16)]
            right = jnp.concatenate(right, axis=1)
            writes = mm(ks[j], right, TN)
            reads = mm(looks[j], right)
            for r in range(REP):
                h = j * REP + r
                at = slice(2 * r * DV, (2 * r + 1) * DV)
                off = slice((2 * r + 1) * DV, (2 * r + 2) * DV)
                rows = jnp.broadcast_to(shrink[:, h : h + 1], (CH, DV))
                moved = at_end[h : h + 1] * writes[:, at]
                if hs.start + h >= first_short:
                    x_step[hs.start + h - first_short] = moved
                step_ref[hs.start + h] = jnp.concatenate(
                    [
                        moved.astype(BF16),
                        (rows * (at_mid[h : h + 1] * (qs[j].astype(F32) + reads[:, at]))).astype(BF16),
                    ],
                    axis=0,
                )
                outbox[hs.start + h] = from_mid[h : h + 1] * writes[:, off]
                seen_ref[hs.start + h] = rows * reads[:, off]
                fade_ref[hs.start + h] = jnp.broadcast_to(at_end[h : h + 1], (8, DV))

    def show(h, o):
        at = pl.ds(pl.multiple_of(h * DV, DV), DV)
        pout[0, :, at] = norm_rows(o, gain_ref[...]).astype(BF16)
        save_prompt(h).start()

    def step_forward(i):
        @pl.when(rank == 0)
        def _():
            show(i, seen_ref[i])

        @pl.when(rank > 0)
        def _():
            forward(i).wait_recv()
            state = inbox[i]
            both = mm(step_ref[i], state.astype(BF16))
            grown = fade_ref[i, :1] * state + both[:DK] + outbox[i]

            @pl.when(rank < last)
            def _():
                outbox[i] = grown
                forward(i).start()

            @pl.when((rank == last - 1) & (i >= first_short))
            def _():
                n = i - first_short
                for part in range(3):
                    lend(n, part).wait_recv()
                finals[mine, i] = (
                    x_near_fade[n, :1] * grown
                    + mm(x_near_step[n].astype(BF16), grown.astype(BF16))
                    + x_near_base[n]
                )
                across(mine, i).start()
                backward(i).start()

            @pl.when(rank == last)
            def _():
                finals[mine, i] = grown
                across(mine, i).start()
                pl.when(i < first_short)(lambda: backward(i).start())

            show(i, both[DK:] + seen_ref[i])

    def step_back(i):
        @pl.when((rank < last - 1) | ((rank == last - 1) & (i < first_short)))
        def _():
            backward(i).wait_recv()

            @pl.when(rank > 0)
            def _():
                backward(i).start()

            across(mine, i).start()

    def step_work(m):
        place, g = m // packs, m % packs
        s, c = place // spans, place % spans
        rows = pl.ds(pl.multiple_of(c * CH, CH), CH)
        if packs > 1:
            hs = pl.ds(pl.multiple_of(g * pack * REP, pack * REP), pack * REP)
        else:
            hs = slice(None)
        at = pl.ds(pl.multiple_of(g * pack * DK, pack * DK), pack * DK)
        log_row, log_back = running_log(sdecay[s, hs, rows], cum)
        beta = spread_beta(sbeta[s, hs, rows], masks)
        betas = [beta[h * SB : (h + 1) * SB] for h in range(pack * REP)]
        grow = (-jnp.exp(-log_row), -jnp.exp(-log_back))
        eps = (EPS_NORM * jnp.exp(-2.0 * log_row)).T
        end = jnp.exp(log_row[:, CH - 1 :])
        q, k = sq[s, rows, at], sk[s, rows, at]
        qs, ks, backs, looks, (first, second) = solve(
            [q[:, j * DK : (j + 1) * DK] for j in range(pack)],
            [k[:, j * DK : (j + 1) * DK] for j in range(pack)],
            betas, masks, pick,
        )
        for j in range(pack):
            to = g * pack + j
            s_key[s, c, to] = ks[j]
            s_look[s, c, to] = jnp.concatenate([qs[j], looks[j]], axis=1)
            s_eps[s, c, to] = eps[:, j * REP : (j + 1) * REP]
            for r, left in enumerate((first[j], second[j])):
                h = j * REP + r
                scaled = (left.astype(F32) * grow[r][h : h + 1]).astype(BF16)
                s_left[s, c, to * REP + r] = jnp.concatenate([scaled, left], axis=1)
                s_end[s, c, to * REP + r] = jnp.broadcast_to(end[h : h + 1], (8, DV))

    lengths, owners = [], []
    for s in range(slots):
        branch = slot_branch[(rank * lax.axis_size("prompt") + mine) * slots + s]
        lengths.append(branch_length[branch])
        owners.append(branch_prompt[branch])

    def step_apply(j):
        at = pl.ds(pl.multiple_of(j * REP * DV, REP * DV), REP * DV)
        place = lax.broadcasted_iota(jnp.int32, (CH, 1), 0)
        gain = gain_ref[...]
        states = [
            [
                jnp.where(owners[s] == 0, finals[0, j * REP + r], finals[1, j * REP + r])
                for r in range(REP)
            ]
            for s in range(slots)
        ]
        for c in range(spans):
            span = slice(c * CH, (c + 1) * CH)
            narrow = [
                jnp.concatenate([x.astype(BF16) for x in states[s]], axis=1) for s in range(slots)
            ]
            reads = [mm(s_key[s, c, j], narrow[s]).astype(BF16) for s in range(slots)]
            news = []
            for s in range(slots):
                v = sv[s, span, at]
                pair = []
                for r in range(REP):
                    cut = slice(r * DV, (r + 1) * DV)
                    a, b = v[:, cut], reads[s][:, cut]
                    if r:
                        a, b = flip(a), flip(b)
                    pair.append(
                        mm(s_left[s, c, j * REP + r], jnp.concatenate([a, b], axis=0)).astype(BF16)
                    )
                news.append(jnp.concatenate(pair, axis=1))
            if c + 1 < spans:
                for s in range(slots):
                    added = mm(s_key[s, c, j], news[s], TN)
                    states[s] = [
                        s_end[s, c, j * REP + r, :1]
                        * (states[s][r] + added[:, r * DV : (r + 1) * DV])
                        for r in range(REP)
                    ]
            for s in range(slots):
                o = mm(s_look[s, c, j], jnp.concatenate([narrow[s], news[s]], axis=0))
                live = place + c * CH < lengths[s]
                normed = []
                for r in range(REP):
                    x = o[:, r * DV : (r + 1) * DV]
                    eps = s_eps[s, c, j, :, r : r + 1]
                    scale = lax.rsqrt(jnp.mean(x * x, axis=-1, keepdims=True) + eps)
                    normed.append((x * jnp.where(live, scale, 0.0) * gain).astype(BF16))
                sout[s, span, at] = jnp.concatenate(normed, axis=1)

    for g in range(packs):
        prepare(g)
        if g == 0:
            meet()

        @pl.when(rank == 0)
        def _():
            for h in range(g * pack * REP, (g + 1) * pack * REP):
                forward(h).start()

        @pl.when(rank == last)
        def _():
            for h in range(max(g * pack * REP, first_short), (g + 1) * pack * REP):
                for part in range(3):
                    lend(h - first_short, part).start()

    for name in LAST_LOADS:
        load(name).wait()

    items = slots * spans * packs
    first_at = LAG * rank
    back_at = LAG * last + BACK * (last - rank) + 1
    apply_at = back_at + AFTER

    def tick(t, carry):
        i = t - first_at
        pl.when((i >= 0) & (i < heads))(lambda: step_forward(i))
        j = t - back_at
        pl.when((j >= 0) & (j < heads))(lambda: step_back(j))
        pl.when(t < items)(lambda: step_work(t))
        a = t - apply_at

        @pl.when((a >= 0) & (a < heads) & (a % REP == REP - 1))
        def _():
            for r in range(REP):
                across(other, a - r).wait_recv()
            step_apply(a // REP)
            save_slot(a // REP).start()

        return carry

    lax.fori_loop(0, max(items, (LAG + BACK) * last + 1 + AFTER + heads), tick, 0)

    def finish(i, carry):
        @pl.when(rank < last)
        def _():
            forward(i).wait_send()

        @pl.when((rank > 0) & ((rank < last) | (i < first_short)))
        def _():
            backward(i).wait_send()

        across(mine, i).wait_send()
        save_prompt(i).wait()
        pl.when(i < key_heads)(lambda: save_slot(i).wait())
        return carry

    lax.fori_loop(0, heads, finish, 0)

    @pl.when(rank == last)
    def _():
        for n in range(short):
            for part in range(3):
                lend(n, part).wait_send()


LOADED = (
    "pq", "pk", "pv", "pbeta", "pdecay", "sq", "sk", "sv", "sbeta", "sdecay",
    "gain", "masks", "cum", "pick",
)
FIRST_LOADS = ("pdecay", "pbeta", "cum", "masks", "pk", "pq", "pick", "pv", "gain")
LAST_LOADS = ("sdecay", "sbeta", "sk", "sq", "sv")
LOAD_ORDER = FIRST_LOADS + LAST_LOADS
SHORT = 1
LAG = 2
BACK = 2
AFTER = 1
PACK = 4


def settle_kernel(count, *refs):
    ins, outs, held = refs[:count], refs[count : 2 * count], refs[2 * count : 3 * count]
    come, go = refs[3 * count :]
    loads, stores = [], []
    for a, b, h in zip(ins, outs, held):
        rows = a.shape[1] // PIECES
        for s in range(a.shape[0]):
            for p in range(PIECES):
                cut = pl.ds(p * rows, rows)
                n = len(loads)
                loads.append(pltpu.make_async_copy(a.at[s, cut], h.at[s, cut], come.at[n]))
                stores.append(pltpu.make_async_copy(h.at[s, cut], b.at[s, cut], go.at[n]))
    for c in loads:
        c.start()
    for c, d in zip(loads, stores):
        c.wait()
        d.start()
    for d in stores:
        d.wait()


def settle(*arrays):
    space = pl.BlockSpec(memory_space=pl.ANY)
    pieces = sum(x.shape[0] for x in arrays) * PIECES
    return pl.pallas_call(
        functools.partial(settle_kernel, len(arrays)),
        out_shape=[jax.ShapeDtypeStruct(x.shape, x.dtype) for x in arrays],
        in_specs=[space] * len(arrays),
        out_specs=[space] * len(arrays),
        scratch_shapes=[pltpu.VMEM(x.shape, x.dtype) for x in arrays]
        + [pltpu.SemaphoreType.DMA((pieces,))] * 2,
        compiler_params=pltpu.CompilerParams(vmem_limit_bytes=60 * 1024 * 1024),
        name="settle",
    )(*arrays)


PIECES = 1


def local(
    prompt_queries, prompt_keys, prompt_values, prompt_beta, prompt_decay,
    suffix_queries, suffix_keys, suffix_values, suffix_beta, suffix_decay,
    norm_gain, slot_branch, branch_length, branch_prompt,
):
    key_heads = prompt_queries.shape[2] // DK
    heads = key_heads * REP
    slots, spans = suffix_queries.shape[0], suffix_queries.shape[1] // CH
    space = pl.BlockSpec(memory_space=pl.ANY)
    smem = pl.BlockSpec(memory_space=pltpu.SMEM)
    short = min(SHORT, heads // 2) if lax.axis_size("seq") > 2 else 0
    state = pltpu.VMEM((heads, DK, DV), F32)
    lent = pltpu.VMEM((short, DK, DV), F32)
    loads = (
        prompt_queries, prompt_keys, prompt_values, prompt_beta, prompt_decay,
        suffix_queries, suffix_keys, suffix_values, suffix_beta, suffix_decay,
        norm_gain[None, :], *(jnp.asarray(x) for x in tables()),
    )
    outs = pl.pallas_call(
        chain_kernel,
        out_shape=[
            jax.ShapeDtypeStruct(prompt_values.shape, BF16),
            jax.ShapeDtypeStruct(suffix_values.shape, BF16),
        ],
        in_specs=[space] * len(loads) + [smem] * 3,
        out_specs=[space] * 2,
        scratch_shapes=[pltpu.VMEM(x.shape, x.dtype) for x in loads]
        + [
            pltpu.VMEM(prompt_values.shape, BF16),
            pltpu.VMEM(suffix_values.shape, BF16),
            pltpu.VMEM((heads, 2 * CH, DK), BF16),
            state,
            pltpu.VMEM((heads, 8, DV), F32),
            state,
            state,
            pltpu.VMEM((2, heads, DK, DV), F32),
            pltpu.VMEM((slots, spans, heads, CH, 2 * CH), BF16),
            pltpu.VMEM((slots, spans, key_heads, CH, 2 * CH), BF16),
            pltpu.VMEM((slots, spans, key_heads, CH, DK), BF16),
            pltpu.VMEM((slots, spans, key_heads, CH, REP), F32),
            pltpu.VMEM((slots, spans, heads, 8, DV), F32),
            lent,
            lent,
            lent,
            pltpu.VMEM((short, 8, DV), F32),
            pltpu.SemaphoreType.DMA((len(loads),)),
            pltpu.SemaphoreType.DMA((heads,)),
            pltpu.SemaphoreType.DMA((key_heads,)),
        ]
        + [pltpu.SemaphoreType.DMA((heads,))] * 6
        + [pltpu.SemaphoreType.DMA((short, 3))] * 2,
        compiler_params=pltpu.CompilerParams(
            collective_id=0, has_side_effects=True, vmem_limit_bytes=56 * 1024 * 1024
        ),
        name="chain",
    )(*loads, slot_branch, branch_length, branch_prompt)
    return tuple(settle(*outs))


def solution(mesh):
    lead = P(("groups", "prompt"), "seq", "head")
    lead_gate = P(("groups", "prompt"), "head", "seq")
    slot = P(("groups", "seq", "prompt"), None, "head")
    slot_gate = P(("groups", "seq", "prompt"), "head", None)
    return jax.shard_map(
        local,
        mesh=mesh,
        in_specs=(
            lead, lead, lead, lead_gate, lead_gate, slot, slot, slot, slot_gate, slot_gate,
            P(), P("groups"), P("groups"), P("groups"),
        ),
        out_specs=(lead, slot),
        check_vma=False,
    )
```

```python
import functools

import jax
import jax.numpy as jnp
import ml_dtypes
import numpy as np
from jax import lax
from jax.experimental import pallas as pl
from jax.experimental.pallas import tpu as pltpu
from jax.sharding import PartitionSpec as P

DK = 128
DV = 128
CH = 128
SB = 16
REP = 2
EPS_NORM = 1e-06
F32 = jnp.float32
BF16 = jnp.bfloat16
MESH = pl.DeviceIdType.MESH
NN = (((1,), (0,)), ((), ()))
NT = (((1,), (1,)), ((), ()))
TN = (((0,), (0,)), ((), ()))

BD = {16: 0, 32: 2, 64: 4}
SWAP = {16: 1, 32: 3, 64: 5}
UPTO, BACKWARDS, THIN = 6, 7, 8
EVEN = {16: 0, 32: 32, 64: 64}
ODD = {16: 16, 32: 48, 64: 80}
STRICT, EYE = 96, 112


def tables():
    l = np.arange(CH)
    r, c = l[:, None], l[None]
    i = np.arange(SB)[:, None]
    squares = []
    for s in (16, 32, 64):
        squares += [r // s == c // s, (r // s) ^ 1 == c // s]
    thin = []
    for s in (16, 32, 64):
        thin += [np.broadcast_to((c // s) % 2 == p, (SB, CH)) for p in (0, 1)]
    thin += [i > c % SB, i == c % SB]
    squares += [r >= c, r ^ (CH - SB) == c, np.concatenate(thin, 0)]
    cum = np.concatenate([r <= c, r <= (c ^ (CH - SB))], 1)
    pick = np.concatenate([r == (c // SB) * SB + k for k in range(SB)], 1)
    b = lambda x: x.astype(np.float32).astype(ml_dtypes.bfloat16)
    return b(np.stack(squares)), b(cum), b(pick)


def mm(a, b, dims=NN):
    return lax.dot_general(a, b, dims, preferred_element_type=F32)


def unit(x):
    w = x.astype(F32)
    return (w * lax.rsqrt(jnp.sum(w * w, axis=-1, keepdims=True) + EPS_NORM)).astype(BF16)


def flip(x):
    return jnp.concatenate([x[i : i + SB] for i in range(CH - SB, -1, -SB)], axis=0)


def tile(x, n):
    return x if n == 1 else jnp.concatenate([x] * n, axis=0)


def terms(x, n):
    parts = []
    for _ in range(n):
        p = x.astype(BF16)
        parts.append(p)
        x = x - p.astype(F32)
    return jnp.concatenate(parts, axis=1)


def running_log(decay, cum):
    both = mm(terms(decay, 3), tile(cum[...], 3))
    return both[:, :CH], both[:, CH:]


def spread_beta(beta, masks):
    eye = masks[THIN, EYE:].astype(F32)
    rows = jnp.concatenate([beta[h : h + 1] * eye for h in range(beta.shape[0])], axis=0)
    return mm(terms(rows, 2), tile(masks[BD[16]], 2))


def small_inverses(grams, betas, masks, pick):
    n = len(grams)
    blocks = CH // SB
    thin = lambda at: masks[THIN, at : at + SB]
    strict = thin(STRICT)
    compact = []
    for g in grams:
        c = g[:SB, :CH] * masks[BD[16], :SB]
        for b in range(1, blocks):
            c = c + g[b * SB : (b + 1) * SB, :CH] * masks[BD[16], b * SB : (b + 1) * SB]
        compact.append(c * strict)
    flat = jnp.concatenate(compact, axis=0)
    eye = thin(EYE).astype(F32)
    top = [-eye[:8]] * (n * REP)
    low = [-eye[8:]] * (n * REP)
    for k in range(SB - 1):
        if k % 2 == 0:
            pair = mm(flat, pick[:, k * CH : (k + 2) * CH])
        e = pair[:, (k % 2) * CH : (k % 2 + 1) * CH]
        for j in range(n):
            for r in range(REP):
                h = j * REP + r
                row = (top[h][k : k + 1] if k < 8 else low[h][k - 8 : k - 7]) * betas[h][k : k + 1]
                if k < 7:
                    top[h] = top[h] - e[j * SB : j * SB + 8] * row
                low[h] = low[h] - e[j * SB + 8 : (j + 1) * SB] * row
    done = [
        (jnp.concatenate([top[h], low[h]], axis=0) * betas[h]).astype(BF16) for h in range(n * REP)
    ]
    first = done[0::2]
    second = mm(jnp.concatenate(done[1::2], axis=0), masks[BACKWARDS]).astype(BF16)
    second = [second[j * SB : (j + 1) * SB] for j in range(n)]
    return first, second


def merge(grams, first, second, masks):
    thin = lambda at: masks[THIN, at : at + SB]
    size = SB
    while size < CH:
        rows = size // SB
        even, odd = tile(thin(EVEN[size]), rows), tile(thin(ODD[size]), rows)
        cross = []
        for g in grams:
            parts = []
            for i in range(rows):
                part = None
                for p in range(CH // (2 * size)):
                    at = (2 * p + 1) * size + i * SB
                    ahead = masks[BD[size], 2 * p * size : 2 * p * size + SB]
                    behind = masks[BD[size], (2 * p + 1) * size : (2 * p + 1) * size + SB]
                    back = CH - SB - (2 * p * size + i * SB)
                    term = g[at : at + SB, :CH] * ahead + g[back : back + SB, CH:] * behind
                    part = term if part is None else part + term
                parts.append(part)
            cross.append(jnp.concatenate(parts, axis=0))
        reps = CH // size
        split = [(a * even, a * odd, b * even, b * odd) for a, b in zip(first, second)]
        mids = [
            mm(c, tile(ae + bo, reps) * masks[BD[size]]).astype(BF16)
            for c, (ae, ao, be, bo) in zip(cross, split)
        ]
        offs = [
            mm(ao + be, tile(m, reps) * masks[SWAP[size]]).astype(BF16)
            for m, (ae, ao, be, bo) in zip(mids, split)
        ]
        first = [
            jnp.concatenate([ae, o * even + ao], axis=0) for o, (ae, ao, be, bo) in zip(offs, split)
        ]
        second = [
            jnp.concatenate([be + o * odd, bo], axis=0) for o, (ae, ao, be, bo) in zip(offs, split)
        ]
        size *= 2
    return first, [flip(x) for x in second]


def grams_of(queries, keys, masks):
    qs, ks = [unit(q) for q in queries], [unit(k) for k in keys]
    backs = [flip(k) for k in ks]
    looks = [mm(q, k, NT).astype(BF16) * masks[UPTO] for q, k in zip(qs, ks)]
    grams = [mm(k, jnp.concatenate([k, b], axis=0), NT).astype(BF16) for k, b in zip(ks, backs)]
    return qs, ks, backs, looks, grams


def norm_rows(o, gain):
    return o * lax.rsqrt(jnp.mean(o * o, axis=-1, keepdims=True) + EPS_NORM) * gain


def chain_kernel(
    *refs,
):
    count = len(LOADED)
    given, facts, (pout, sout) = refs[:count], refs[count : count + 3], refs[count + 3 : count + 5]
    held, rest = refs[count + 5 : 2 * count + 5], refs[2 * count + 5 :]
    pq, pk, pv, pbeta, pdecay, sq, sk, sv, sbeta, sdecay, gain_ref, masks, cum, pick = held
    slot_branch, branch_length, branch_prompt = facts
    (
        step_ref, seen_ref, fade_ref, inbox, outbox, finals,
        s_left, s_look, s_key, s_eps, s_end, g_beta, g_grow, w_gram, w_small,
        load_sem,
        fsend, frecv, bsend, brecv, csend, crecv,
    ) = rest
    key_heads = pq.shape[2] // DK
    heads = key_heads * REP
    slots, spans = sq.shape[0], sq.shape[1] // CH
    pack = PACK if key_heads % PACK == 0 else key_heads
    packs = key_heads // pack
    rank, last = lax.axis_index("seq"), lax.axis_size("seq") - 1
    mine = lax.axis_index("prompt")
    other = 1 - mine

    def load(name):
        n = LOADED.index(name)
        return pltpu.make_async_copy(given[n], held[n], load_sem.at[n])

    for name in LOAD_ORDER:
        load(name).start()

    def forward(i):
        return pltpu.make_async_remote_copy(
            src_ref=outbox.at[i], dst_ref=inbox.at[i], send_sem=fsend.at[i],
            recv_sem=frecv.at[i], device_id={"seq": rank + 1}, device_id_type=MESH,
        )

    def backward(i):
        return pltpu.make_async_remote_copy(
            src_ref=finals.at[mine, i], dst_ref=finals.at[mine, i], send_sem=bsend.at[i],
            recv_sem=brecv.at[i], device_id={"seq": rank - 1}, device_id_type=MESH,
        )

    def across(p, i):
        return pltpu.make_async_remote_copy(
            src_ref=finals.at[p, i], dst_ref=finals.at[p, i], send_sem=csend.at[i],
            recv_sem=crecv.at[i], device_id={"prompt": other}, device_id_type=MESH,
        )

    barrier = pltpu.get_barrier_semaphore()

    def greet(where):
        pl.semaphore_signal(barrier, inc=1, device_id=where, device_id_type=MESH)

    greet({"prompt": other})

    @pl.when(rank > 0)
    def _():
        greet({"seq": rank - 1})

    @pl.when(rank < last)
    def _():
        greet({"seq": rank + 1})

    def meet():
        pl.semaphore_wait(barrier, 1 + jnp.where(rank > 0, 1, 0) + jnp.where(rank < last, 1, 0))

    for name in FIRST_LOADS:
        load(name).wait()

    def prepare(g, size):
        cols = [slice(j * DK, (j + 1) * DK) for j in range(g, g + size)]
        hs = slice(g * REP, (g + size) * REP)
        log_row, log_back = running_log(pdecay[0, hs], cum)
        beta = spread_beta(pbeta[0, hs], masks)
        betas = [beta[h * SB : (h + 1) * SB] for h in range(size * REP)]
        mid = log_row[:, CH // 2 - 1 : CH // 2]
        end = log_row[:, CH - 1 :]
        grow = (-jnp.exp(mid - log_row), -jnp.exp(mid - log_back))
        from_mid = jnp.exp(end - mid)
        qs, ks, backs, looks, grams = grams_of(
            [pq[0, :, c] for c in cols], [pk[0, :, c] for c in cols], masks
        )
        first, second = merge(grams, *small_inverses(grams, betas, masks, pick), masks)
        rights = []
        for j in range(size):
            right = []
            for r, left in enumerate((first[j], second[j])):
                h = j * REP + r
                v = pv[0, :, (hs.start + h) * DV : (hs.start + h + 1) * DV]
                scaled = (left.astype(F32) * grow[r][h : h + 1]).astype(BF16)
                right.append(mm(scaled, flip(v) if r else v).astype(BF16))
            rights.append(jnp.concatenate(right, axis=1))
            writes = mm(ks[j], rights[j], TN)
            for r in range(REP):
                h = j * REP + r
                outbox[hs.start + h] = from_mid[h : h + 1] * writes[:, r * DV : (r + 1) * DV]

        def rest():
            shrink = jnp.exp(log_row - mid).T
            at_mid, at_end = jnp.exp(mid), jnp.exp(end)
            for j in range(size):
                turn = jnp.concatenate(
                    [mm(first[j], ks[j]).astype(BF16), mm(second[j], backs[j]).astype(BF16)], axis=1
                )
                moves = mm(ks[j], turn, TN)
                reads = mm(looks[j], jnp.concatenate([turn, rights[j]], axis=1))
                for r in range(REP):
                    h = j * REP + r
                    cut, off = slice(r * DV, (r + 1) * DV), slice((REP + r) * DV, (REP + r + 1) * DV)
                    rows = jnp.broadcast_to(shrink[:, h : h + 1], (CH, DV))
                    step_ref[hs.start + h] = jnp.concatenate(
                        [
                            (at_end[h : h + 1] * moves[:, cut]).astype(BF16),
                            (
                                rows * (at_mid[h : h + 1] * (qs[j].astype(F32) + reads[:, cut]))
                            ).astype(BF16),
                        ],
                        axis=0,
                    )
                    seen_ref[hs.start + h] = rows * reads[:, off]
                    fade_ref[hs.start + h] = jnp.broadcast_to(at_end[h : h + 1], (8, DV))

        return rest

    def show(h, o):
        at = pl.ds(pl.multiple_of(h * DV, DV), DV)
        pout[0, :, at] = norm_rows(o, gain_ref[...]).astype(BF16)

    def step_forward(i):
        @pl.when(rank == 0)
        def _():
            show(i, seen_ref[i])

        @pl.when(rank > 0)
        def _():
            forward(i).wait_recv()
            state = inbox[i]
            both = mm(step_ref[i], state.astype(BF16))
            grown = fade_ref[i, :1] * state + both[:DK] + outbox[i]

            @pl.when(rank < last)
            def _():
                outbox[i] = grown
                forward(i).start()

            @pl.when(rank == last)
            def _():
                finals[mine, i] = grown
                across(mine, i).start()
                backward(i).start()

            show(i, both[DK:] + seen_ref[i])

    def step_back(i):
        @pl.when(rank < last)
        def _():
            backward(i).wait_recv()

            @pl.when(rank > 0)
            def _():
                backward(i).start()

            across(mine, i).start()

    def gates(s, c):
        span = slice(c * CH, (c + 1) * CH)
        log_row, log_back = running_log(sdecay[s, :, span], cum)
        beta = spread_beta(sbeta[s, :, span], masks)
        grow = (-jnp.exp(-log_row), -jnp.exp(-log_back))
        eps = (EPS_NORM * jnp.exp(-2.0 * log_row)).T
        end = jnp.exp(log_row[:, CH - 1 :])
        for h in range(heads):
            g_beta[s, c, h] = beta[h * SB : (h + 1) * SB]
            g_grow[s, c, h] = jnp.broadcast_to(grow[h % REP][h : h + 1], (8, CH))
            s_end[s, c, h] = jnp.broadcast_to(end[h : h + 1], (8, DV))
        for j in range(key_heads):
            s_eps[s, c, j] = eps[:, j * REP : (j + 1) * REP]

    def where_of(m):
        g, place = m // (slots * spans), m % (slots * spans)
        return place // spans, place % spans, g

    def work_grams(m):
        s, c, g = where_of(m)
        rows = pl.ds(pl.multiple_of(c * CH, CH), CH)
        at = pl.ds(pl.multiple_of(g * pack * DK, pack * DK), pack * DK)
        q, k = sq[s, rows, at], sk[s, rows, at]
        qs, ks, backs, looks, grams = grams_of(
            [q[:, j * DK : (j + 1) * DK] for j in range(pack)],
            [k[:, j * DK : (j + 1) * DK] for j in range(pack)],
            masks,
        )
        betas = [g_beta[s, c, g * pack * REP + h] for h in range(pack * REP)]
        first, second = small_inverses(grams, betas, masks, pick)
        for j in range(pack):
            to = g * pack + j
            s_key[s, c, to] = ks[j]
            s_look[s, c, to] = jnp.concatenate([qs[j], looks[j]], axis=1)
            w_gram[j] = grams[j]
            w_small[j] = jnp.concatenate([first[j], second[j]], axis=0)

    def work_merge(m):
        s, c, g = where_of(m)
        first, second = merge(
            [w_gram[j] for j in range(pack)],
            [w_small[j, :SB] for j in range(pack)],
            [w_small[j, SB:] for j in range(pack)],
            masks,
        )
        for j in range(pack):
            for r, left in enumerate((first[j], second[j])):
                h = (g * pack + j) * REP + r
                scaled = (left.astype(F32) * g_grow[s, c, h, :1]).astype(BF16)
                s_left[s, c, h] = jnp.concatenate([scaled, left], axis=1)

    def quantum(w):
        pl.when(w % 2 == 0)(lambda: work_grams(w // 2))
        pl.when(w % 2 == 1)(lambda: work_merge(w // 2))

    lengths, owners = [], []
    for s in range(slots):
        branch = slot_branch[(rank * lax.axis_size("prompt") + mine) * slots + s]
        lengths.append(branch_length[branch])
        owners.append(branch_prompt[branch])

    def step_apply(j):
        at = pl.ds(pl.multiple_of(j * REP * DV, REP * DV), REP * DV)
        place = lax.broadcasted_iota(jnp.int32, (CH, 1), 0)
        gain = gain_ref[...]
        states = [
            [
                jnp.where(owners[s] == 0, finals[0, j * REP + r], finals[1, j * REP + r])
                for r in range(REP)
            ]
            for s in range(slots)
        ]
        for c in range(spans):
            span = slice(c * CH, (c + 1) * CH)
            narrow = [
                jnp.concatenate([x.astype(BF16) for x in states[s]], axis=1) for s in range(slots)
            ]
            reads = [mm(s_key[s, c, j], narrow[s]).astype(BF16) for s in range(slots)]
            news = []
            for s in range(slots):
                v = sv[s, span, at]
                pair = []
                for r in range(REP):
                    cut = slice(r * DV, (r + 1) * DV)
                    a, b = v[:, cut], reads[s][:, cut]
                    if r:
                        a, b = flip(a), flip(b)
                    pair.append(
                        mm(s_left[s, c, j * REP + r], jnp.concatenate([a, b], axis=0)).astype(BF16)
                    )
                news.append(jnp.concatenate(pair, axis=1))
            if c + 1 < spans:
                for s in range(slots):
                    added = mm(s_key[s, c, j], news[s], TN)
                    states[s] = [
                        s_end[s, c, j * REP + r, :1]
                        * (states[s][r] + added[:, r * DV : (r + 1) * DV])
                        for r in range(REP)
                    ]
            for s in range(slots):
                o = mm(s_look[s, c, j], jnp.concatenate([narrow[s], news[s]], axis=0))
                live = place + c * CH < lengths[s]
                normed = []
                for r in range(REP):
                    x = o[:, r * DV : (r + 1) * DV]
                    eps = s_eps[s, c, j, :, r : r + 1]
                    scale = lax.rsqrt(jnp.mean(x * x, axis=-1, keepdims=True) + eps)
                    normed.append((x * jnp.where(live, scale, 0.0) * gain).astype(BF16))
                sout[s, span, at] = jnp.concatenate(normed, axis=1)

    size = FIRST if key_heads % FIRST == 0 else key_heads
    later = []
    for g in range(0, key_heads, size):
        later.append(prepare(g, size))
        if g == 0:
            meet()

        @pl.when(rank == 0)
        def _():
            for h in range(g * REP, (g + size) * REP):
                forward(h).start()

    for rest in later:
        rest()

    for name in LAST_LOADS:
        load(name).wait()

    for g in range(slots):
        for c in range(spans):
            gates(g, c)

    quanta = 2 * slots * spans * packs
    early = jnp.where(rank == 0, quanta, jnp.minimum(EARLY * (rank - 1), quanta))
    lax.fori_loop(0, early, lambda w, x: (quantum(w), x)[1], 0)
    back_lag = BACK * (last - rank)
    apply_lag = back_lag + AFTER

    def tick(t, carry):
        pl.when(t < heads)(lambda: step_forward(t))
        j = t - back_lag
        pl.when((j >= 0) & (j < heads))(lambda: step_back(j))
        w = t + early
        pl.when(w < quanta)(lambda: quantum(w))
        a = t - apply_lag

        @pl.when((a >= 0) & (a < heads) & (a % REP == REP - 1))
        def _():
            for r in range(REP):
                across(other, a - r).wait_recv()
            step_apply(a // REP)

        return carry

    lax.fori_loop(0, jnp.maximum(heads + apply_lag, quanta - early), tick, 0)

    def finish(i, carry):
        @pl.when(rank < last)
        def _():
            forward(i).wait_send()

        @pl.when(rank > 0)
        def _():
            backward(i).wait_send()

        across(mine, i).wait_send()
        return carry

    lax.fori_loop(0, heads, finish, 0)


LOADED = (
    "pq", "pk", "pv", "pbeta", "pdecay", "sq", "sk", "sv", "sbeta", "sdecay",
    "gain", "masks", "cum", "pick",
)
FIRST_LOADS = ("pdecay", "pbeta", "cum", "masks", "pk", "pq", "pick", "pv", "gain")
LAST_LOADS = ("sdecay", "sbeta", "sk", "sq", "sv")
LOAD_ORDER = FIRST_LOADS + LAST_LOADS
BACK = 5
AFTER = 2
EARLY = 3
FIRST = 8
PACK = 8


def settle_kernel(count, *refs):
    copies = [
        pltpu.make_async_copy(a, b, refs[2 * count].at[n])
        for n, (a, b) in enumerate(zip(refs[:count], refs[count : 2 * count]))
    ]
    for c in copies:
        c.start()
    for c in copies:
        c.wait()


def settle(*arrays):
    count = len(arrays)
    return pl.pallas_call(
        functools.partial(settle_kernel, count),
        out_shape=[jax.ShapeDtypeStruct(x.shape, x.dtype) for x in arrays],
        in_specs=[pl.BlockSpec(memory_space=pltpu.VMEM)] * count,
        out_specs=[pl.BlockSpec(memory_space=pl.ANY)] * count,
        scratch_shapes=[pltpu.SemaphoreType.DMA((count,))],
        compiler_params=pltpu.CompilerParams(vmem_limit_bytes=8 * 1024 * 1024),
        name="settle",
    )(*arrays)


def local(
    prompt_queries, prompt_keys, prompt_values, prompt_beta, prompt_decay,
    suffix_queries, suffix_keys, suffix_values, suffix_beta, suffix_decay,
    norm_gain, slot_branch, branch_length, branch_prompt,
):
    key_heads = prompt_queries.shape[2] // DK
    heads = key_heads * REP
    slots, spans = suffix_queries.shape[0], suffix_queries.shape[1] // CH
    space = pl.BlockSpec(memory_space=pl.ANY)
    smem = pl.BlockSpec(memory_space=pltpu.SMEM)
    pack = PACK if key_heads % PACK == 0 else key_heads
    state = pltpu.VMEM((heads, DK, DV), F32)
    loads = (
        prompt_queries, prompt_keys, prompt_values, prompt_beta, prompt_decay,
        suffix_queries, suffix_keys, suffix_values, suffix_beta, suffix_decay,
        norm_gain[None, :], *(jnp.asarray(x) for x in tables()),
    )
    outs = pl.pallas_call(
        chain_kernel,
        out_shape=[
            pltpu.VMEM(prompt_values.shape, BF16),
            pltpu.VMEM(suffix_values.shape, BF16),
        ],
        in_specs=[space] * len(loads) + [smem] * 3,
        out_specs=[pl.BlockSpec(memory_space=pltpu.VMEM)] * 2,
        scratch_shapes=[pltpu.VMEM(x.shape, x.dtype) for x in loads]
        + [
            pltpu.VMEM((heads, 2 * CH, DK), BF16),
            state,
            pltpu.VMEM((heads, 8, DV), F32),
            state,
            state,
            pltpu.VMEM((2, heads, DK, DV), F32),
            pltpu.VMEM((slots, spans, heads, CH, 2 * CH), BF16),
            pltpu.VMEM((slots, spans, key_heads, CH, 2 * CH), BF16),
            pltpu.VMEM((slots, spans, key_heads, CH, DK), BF16),
            pltpu.VMEM((slots, spans, key_heads, CH, REP), F32),
            pltpu.VMEM((slots, spans, heads, 8, DV), F32),
            pltpu.VMEM((slots, spans, heads, SB, CH), F32),
            pltpu.VMEM((slots, spans, heads, 8, CH), F32),
            pltpu.VMEM((pack, CH, 2 * CH), BF16),
            pltpu.VMEM((pack, 2 * SB, CH), BF16),
            pltpu.SemaphoreType.DMA((len(loads),)),
        ]
        + [pltpu.SemaphoreType.DMA((heads,))] * 6,
        compiler_params=pltpu.CompilerParams(
            collective_id=0, has_side_effects=True, vmem_limit_bytes=60 * 1024 * 1024
        ),
        name="chain",
    )(*loads, slot_branch, branch_length, branch_prompt)
    return tuple(settle(*outs))


def solution(mesh):
    lead = P(("groups", "prompt"), "seq", "head")
    lead_gate = P(("groups", "prompt"), "head", "seq")
    slot = P(("groups", "seq", "prompt"), None, "head")
    slot_gate = P(("groups", "seq", "prompt"), "head", None)
    return jax.shard_map(
        local,
        mesh=mesh,
        in_specs=(
            lead, lead, lead, lead_gate, lead_gate, slot, slot, slot, slot_gate, slot_gate,
            P(), P("groups"), P("groups"), P("groups"),
        ),
        out_specs=(lead, slot),
        check_vma=False,
    )
```

```python
import functools

import jax
import jax.numpy as jnp
import ml_dtypes
import numpy as np
from jax import lax
from jax.experimental import pallas as pl
from jax.experimental.pallas import tpu as pltpu
from jax.sharding import PartitionSpec as P

DK = 128
DV = 128
CH = 128
SB = 16
REP = 2
EPS_NORM = 1e-06
F32 = jnp.float32
BF16 = jnp.bfloat16
MESH = pl.DeviceIdType.MESH
NN = (((1,), (0,)), ((), ()))
NT = (((1,), (1,)), ((), ()))
TN = (((0,), (0,)), ((), ()))

BD = {16: 0, 32: 2, 64: 4}
SWAP = {16: 1, 32: 3, 64: 5}
UPTO, BACKWARDS, THIN = 6, 7, 8
EVEN = {16: 0, 32: 32, 64: 64}
ODD = {16: 16, 32: 48, 64: 80}
STRICT, EYE = 96, 112


def tables():
    l = np.arange(CH)
    r, c = l[:, None], l[None]
    i = np.arange(SB)[:, None]
    squares = []
    for s in (16, 32, 64):
        squares += [r // s == c // s, (r // s) ^ 1 == c // s]
    thin = []
    for s in (16, 32, 64):
        thin += [np.broadcast_to((c // s) % 2 == p, (SB, CH)) for p in (0, 1)]
    thin += [i > c % SB, i == c % SB]
    squares += [r >= c, r ^ (CH - SB) == c, np.concatenate(thin, 0)]
    cum = np.concatenate([r <= c, r <= (c ^ (CH - SB))], 1)
    pick = np.concatenate([r == (c // SB) * SB + k for k in range(SB)], 1)
    b = lambda x: x.astype(np.float32).astype(ml_dtypes.bfloat16)
    return b(np.stack(squares)), b(cum), b(pick)


def mm(a, b, dims=NN):
    return lax.dot_general(a, b, dims, preferred_element_type=F32)


def unit(x):
    w = x.astype(F32)
    return (w * lax.rsqrt(jnp.sum(w * w, axis=-1, keepdims=True) + EPS_NORM)).astype(BF16)


def flip(x):
    return jnp.concatenate([x[i : i + SB] for i in range(CH - SB, -1, -SB)], axis=0)


def tile(x, n):
    return x if n == 1 else jnp.concatenate([x] * n, axis=0)


def terms(x, n):
    parts = []
    for _ in range(n):
        p = x.astype(BF16)
        parts.append(p)
        x = x - p.astype(F32)
    return jnp.concatenate(parts, axis=1)


def running_log(decay, cum):
    both = mm(terms(decay, 3), tile(cum[...], 3))
    return both[:, :CH], both[:, CH:]


def spread_beta(beta, masks):
    eye = masks[THIN, EYE:].astype(F32)
    rows = jnp.concatenate([beta[h : h + 1] * eye for h in range(beta.shape[0])], axis=0)
    return mm(terms(rows, 2), tile(masks[BD[16]], 2))


def small_inverses(grams, betas, masks, pick):
    n = len(grams)
    blocks = CH // SB
    thin = lambda at: masks[THIN, at : at + SB]
    strict = thin(STRICT)
    compact = []
    for g in grams:
        c = g[:SB, :CH] * masks[BD[16], :SB]
        for b in range(1, blocks):
            c = c + g[b * SB : (b + 1) * SB, :CH] * masks[BD[16], b * SB : (b + 1) * SB]
        compact.append(c * strict)
    flat = jnp.concatenate(compact, axis=0)
    eye = thin(EYE).astype(F32)
    top = [-eye[:8]] * (n * REP)
    low = [-eye[8:]] * (n * REP)
    for k in range(SB - 1):
        if k % 2 == 0:
            pair = mm(flat, pick[:, k * CH : (k + 2) * CH])
        e = pair[:, (k % 2) * CH : (k % 2 + 1) * CH]
        for j in range(n):
            for r in range(REP):
                h = j * REP + r
                row = (top[h][k : k + 1] if k < 8 else low[h][k - 8 : k - 7]) * betas[h][k : k + 1]
                if k < 7:
                    top[h] = top[h] - e[j * SB : j * SB + 8] * row
                low[h] = low[h] - e[j * SB + 8 : (j + 1) * SB] * row
    done = [
        (jnp.concatenate([top[h], low[h]], axis=0) * betas[h]).astype(BF16) for h in range(n * REP)
    ]
    first = done[0::2]
    second = mm(jnp.concatenate(done[1::2], axis=0), masks[BACKWARDS]).astype(BF16)
    second = [second[j * SB : (j + 1) * SB] for j in range(n)]
    return first, second


def merge(grams, first, second, masks):
    thin = lambda at: masks[THIN, at : at + SB]
    size = SB
    while size < CH:
        rows = size // SB
        even, odd = tile(thin(EVEN[size]), rows), tile(thin(ODD[size]), rows)
        cross = []
        for g in grams:
            parts = []
            for i in range(rows):
                part = None
                for p in range(CH // (2 * size)):
                    at = (2 * p + 1) * size + i * SB
                    ahead = masks[BD[size], 2 * p * size : 2 * p * size + SB]
                    behind = masks[BD[size], (2 * p + 1) * size : (2 * p + 1) * size + SB]
                    back = CH - SB - (2 * p * size + i * SB)
                    term = g[at : at + SB, :CH] * ahead + g[back : back + SB, CH:] * behind
                    part = term if part is None else part + term
                parts.append(part)
            cross.append(jnp.concatenate(parts, axis=0))
        reps = CH // size
        split = [(a * even, a * odd, b * even, b * odd) for a, b in zip(first, second)]
        mids = [
            mm(c, tile(ae + bo, reps) * masks[BD[size]]).astype(BF16)
            for c, (ae, ao, be, bo) in zip(cross, split)
        ]
        offs = [
            mm(ao + be, tile(m, reps) * masks[SWAP[size]]).astype(BF16)
            for m, (ae, ao, be, bo) in zip(mids, split)
        ]
        first = [
            jnp.concatenate([ae, o * even + ao], axis=0) for o, (ae, ao, be, bo) in zip(offs, split)
        ]
        second = [
            jnp.concatenate([be + o * odd, bo], axis=0) for o, (ae, ao, be, bo) in zip(offs, split)
        ]
        size *= 2
    return first, [flip(x) for x in second]


def grams_of(queries, keys, masks):
    qs, ks = [unit(q) for q in queries], [unit(k) for k in keys]
    backs = [flip(k) for k in ks]
    looks = [mm(q, k, NT).astype(BF16) * masks[UPTO] for q, k in zip(qs, ks)]
    grams = [mm(k, jnp.concatenate([k, b], axis=0), NT).astype(BF16) for k, b in zip(ks, backs)]
    return qs, ks, backs, looks, grams


def norm_rows(o, gain):
    return o * lax.rsqrt(jnp.mean(o * o, axis=-1, keepdims=True) + EPS_NORM) * gain


def chain_kernel(
    *refs,
):
    count = len(LOADED)
    given, facts, (pout, sout) = refs[:count], refs[count : count + 3], refs[count + 3 : count + 5]
    held, rest = refs[count + 5 : 2 * count + 5], refs[2 * count + 5 :]
    pq, pk, pv, pbeta, pdecay, sq, sk, sv, sbeta, sdecay, gain_ref, masks, cum, pick = held
    (
        step_ref, seen_ref, fade_ref, inbox, outbox, finals,
        s_left, s_look, s_key, s_eps, s_end, g_beta, g_grow, w_gram, w_small,
        *told, load_sem, fact_sem,
        fsend, frecv, bsend, brecv, csend, crecv,
    ) = rest
    slot_branch, branch_length, branch_prompt = told
    key_heads = pq.shape[2] // DK
    heads = key_heads * REP
    slots, spans = sq.shape[0], sq.shape[1] // CH
    pack = PACK if key_heads % PACK == 0 else key_heads
    packs = key_heads // pack
    rank, last = lax.axis_index("seq"), lax.axis_size("seq") - 1
    mine = lax.axis_index("prompt")
    other = 1 - mine

    def load(name):
        n = LOADED.index(name)
        return pltpu.make_async_copy(given[n], held[n], load_sem.at[n])

    for name in LOAD_ORDER:
        load(name).start()
    tell = [
        pltpu.make_async_copy(a, b, fact_sem.at[n]) for n, (a, b) in enumerate(zip(facts, told))
    ]
    for c in tell:
        c.start()

    def forward(i):
        return pltpu.make_async_remote_copy(
            src_ref=outbox.at[i], dst_ref=inbox.at[i], send_sem=fsend.at[i],
            recv_sem=frecv.at[i], device_id={"seq": rank + 1}, device_id_type=MESH,
        )

    def backward(i):
        return pltpu.make_async_remote_copy(
            src_ref=finals.at[mine, i], dst_ref=finals.at[mine, i], send_sem=bsend.at[i],
            recv_sem=brecv.at[i], device_id={"seq": rank - 1}, device_id_type=MESH,
        )

    def across(p, i):
        return pltpu.make_async_remote_copy(
            src_ref=finals.at[p, i], dst_ref=finals.at[p, i], send_sem=csend.at[i],
            recv_sem=crecv.at[i], device_id={"prompt": other}, device_id_type=MESH,
        )

    barrier = pltpu.get_barrier_semaphore()

    def greet(where):
        pl.semaphore_signal(barrier, inc=1, device_id=where, device_id_type=MESH)

    greet({"prompt": other})

    @pl.when(rank > 0)
    def _():
        greet({"seq": rank - 1})

    @pl.when(rank < last)
    def _():
        greet({"seq": rank + 1})


    def meet():
        pl.semaphore_wait(barrier, 1 + jnp.where(rank > 0, 1, 0) + jnp.where(rank < last, 1, 0))

    for name in FIRST_LOADS:
        load(name).wait()

    def prepare(g, size):
        cols = [slice(j * DK, (j + 1) * DK) for j in range(g, g + size)]
        hs = slice(g * REP, (g + size) * REP)
        log_row, log_back = running_log(pdecay[0, hs], cum)
        beta = spread_beta(pbeta[0, hs], masks)
        betas = [beta[h * SB : (h + 1) * SB] for h in range(size * REP)]
        mid = log_row[:, CH // 2 - 1 : CH // 2]
        end = log_row[:, CH - 1 :]
        grow = (-jnp.exp(mid - log_row), -jnp.exp(mid - log_back))
        from_mid = jnp.exp(end - mid)
        qs, ks, backs, looks, grams = grams_of(
            [pq[0, :, c] for c in cols], [pk[0, :, c] for c in cols], masks
        )
        first, second = merge(grams, *small_inverses(grams, betas, masks, pick), masks)
        rights = []
        for j in range(size):
            right = []
            for r, left in enumerate((first[j], second[j])):
                h = j * REP + r
                v = pv[0, :, (hs.start + h) * DV : (hs.start + h + 1) * DV]
                scaled = (left.astype(F32) * grow[r][h : h + 1]).astype(BF16)
                right.append(mm(scaled, flip(v) if r else v).astype(BF16))
            rights.append(jnp.concatenate(right, axis=1))
            writes = mm(ks[j], rights[j], TN)
            for r in range(REP):
                h = j * REP + r
                outbox[hs.start + h] = from_mid[h : h + 1] * writes[:, r * DV : (r + 1) * DV]

        def rest():
            shrink = jnp.exp(log_row - mid).T
            at_mid, at_end = jnp.exp(mid), jnp.exp(end)
            for j in range(size):
                turn = jnp.concatenate(
                    [mm(first[j], ks[j]).astype(BF16), mm(second[j], backs[j]).astype(BF16)], axis=1
                )
                moves = mm(ks[j], turn, TN)
                reads = mm(looks[j], jnp.concatenate([turn, rights[j]], axis=1))
                for r in range(REP):
                    h = j * REP + r
                    cut, off = slice(r * DV, (r + 1) * DV), slice((REP + r) * DV, (REP + r + 1) * DV)
                    rows = jnp.broadcast_to(shrink[:, h : h + 1], (CH, DV))
                    step_ref[hs.start + h] = jnp.concatenate(
                        [
                            (at_end[h : h + 1] * moves[:, cut]).astype(BF16),
                            (
                                rows * (at_mid[h : h + 1] * (qs[j].astype(F32) + reads[:, cut]))
                            ).astype(BF16),
                        ],
                        axis=0,
                    )
                    seen_ref[hs.start + h] = rows * reads[:, off]
                    fade_ref[hs.start + h] = jnp.broadcast_to(at_end[h : h + 1], (8, DV))

        return rest

    def show(h, o):
        at = pl.ds(pl.multiple_of(h * DV, DV), DV)
        pout[0, :, at] = norm_rows(o, gain_ref[...]).astype(BF16)

    def step_forward(i):
        @pl.when(rank == 0)
        def _():
            show(i, seen_ref[i])

        @pl.when(rank > 0)
        def _():
            forward(i).wait_recv()
            state = inbox[i]
            both = mm(step_ref[i], state.astype(BF16))
            grown = fade_ref[i, :1] * state + both[:DK] + outbox[i]

            @pl.when(rank < last)
            def _():
                outbox[i] = grown
                forward(i).start()

            @pl.when(rank == last)
            def _():
                finals[mine, i] = grown
                across(mine, i).start()
                backward(i).start()

            show(i, both[DK:] + seen_ref[i])

    def step_back(i):
        @pl.when(rank < last)
        def _():
            backward(i).wait_recv()

            @pl.when(rank > 0)
            def _():
                backward(i).start()

            across(mine, i).start()

    def gates(s, c):
        span = slice(c * CH, (c + 1) * CH)
        log_row, log_back = running_log(sdecay[s, :, span], cum)
        beta = spread_beta(sbeta[s, :, span], masks)
        grow = (-jnp.exp(-log_row), -jnp.exp(-log_back))
        eps = (EPS_NORM * jnp.exp(-2.0 * log_row)).T
        end = jnp.exp(log_row[:, CH - 1 :])
        for h in range(heads):
            g_beta[s, c, h] = beta[h * SB : (h + 1) * SB]
            g_grow[s, c, h] = jnp.broadcast_to(grow[h % REP][h : h + 1], (8, CH))
            s_end[s, c, h] = jnp.broadcast_to(end[h : h + 1], (8, DV))
        for j in range(key_heads):
            s_eps[s, c, j] = eps[:, j * REP : (j + 1) * REP]

    def where_of(m):
        g, place = m // (slots * spans), m % (slots * spans)
        return place // spans, place % spans, g

    def work_grams(m):
        s, c, g = where_of(m)
        rows = pl.ds(pl.multiple_of(c * CH, CH), CH)
        at = pl.ds(pl.multiple_of(g * pack * DK, pack * DK), pack * DK)
        q, k = sq[s, rows, at], sk[s, rows, at]
        qs, ks, backs, looks, grams = grams_of(
            [q[:, j * DK : (j + 1) * DK] for j in range(pack)],
            [k[:, j * DK : (j + 1) * DK] for j in range(pack)],
            masks,
        )
        betas = [g_beta[s, c, g * pack * REP + h] for h in range(pack * REP)]
        first, second = small_inverses(grams, betas, masks, pick)
        for j in range(pack):
            to = g * pack + j
            s_key[s, c, to] = ks[j]
            s_look[s, c, to] = jnp.concatenate([qs[j], looks[j]], axis=1)
            w_gram[j] = grams[j]
            w_small[j] = jnp.concatenate([first[j], second[j]], axis=0)

    def work_merge(m):
        s, c, g = where_of(m)
        first, second = merge(
            [w_gram[j] for j in range(pack)],
            [w_small[j, :SB] for j in range(pack)],
            [w_small[j, SB:] for j in range(pack)],
            masks,
        )
        for j in range(pack):
            for r, left in enumerate((first[j], second[j])):
                h = (g * pack + j) * REP + r
                scaled = (left.astype(F32) * g_grow[s, c, h, :1]).astype(BF16)
                s_left[s, c, h] = jnp.concatenate([scaled, left], axis=1)

    def quantum(w):
        pl.when(w % 2 == 0)(lambda: work_grams(w // 2))
        pl.when(w % 2 == 1)(lambda: work_merge(w // 2))

    def step_apply(j):
        at = pl.ds(pl.multiple_of(j * REP * DV, REP * DV), REP * DV)
        place = lax.broadcasted_iota(jnp.int32, (CH, 1), 0)
        gain = gain_ref[...]
        states = [
            [
                jnp.where(owners[s] == 0, finals[0, j * REP + r], finals[1, j * REP + r])
                for r in range(REP)
            ]
            for s in range(slots)
        ]
        for c in range(spans):
            span = slice(c * CH, (c + 1) * CH)
            narrow = [
                jnp.concatenate([x.astype(BF16) for x in states[s]], axis=1) for s in range(slots)
            ]
            reads = [mm(s_key[s, c, j], narrow[s]).astype(BF16) for s in range(slots)]
            news = []
            for s in range(slots):
                v = sv[s, span, at]
                pair = []
                for r in range(REP):
                    cut = slice(r * DV, (r + 1) * DV)
                    a, b = v[:, cut], reads[s][:, cut]
                    if r:
                        a, b = flip(a), flip(b)
                    pair.append(
                        mm(s_left[s, c, j * REP + r], jnp.concatenate([a, b], axis=0)).astype(BF16)
                    )
                news.append(jnp.concatenate(pair, axis=1))
            if c + 1 < spans:
                for s in range(slots):
                    added = mm(s_key[s, c, j], news[s], TN)
                    states[s] = [
                        s_end[s, c, j * REP + r, :1]
                        * (states[s][r] + added[:, r * DV : (r + 1) * DV])
                        for r in range(REP)
                    ]
            for s in range(slots):
                o = mm(s_look[s, c, j], jnp.concatenate([narrow[s], news[s]], axis=0))
                live = place + c * CH < lengths[s]
                normed = []
                for r in range(REP):
                    x = o[:, r * DV : (r + 1) * DV]
                    eps = s_eps[s, c, j, :, r : r + 1]
                    scale = lax.rsqrt(jnp.mean(x * x, axis=-1, keepdims=True) + eps)
                    normed.append((x * jnp.where(live, scale, 0.0) * gain).astype(BF16))
                sout[s, span, at] = jnp.concatenate(normed, axis=1)

    size = FIRST if key_heads % FIRST == 0 else key_heads
    later = []
    for g in range(0, key_heads, size):
        later.append(prepare(g, size))
        if g == 0:
            meet()

        @pl.when(rank == 0)
        def _():
            for h in range(g * REP, (g + size) * REP):
                forward(h).start()

    for rest in later:
        rest()

    for c in tell:
        c.wait()
    lengths, owners = [], []
    for s in range(slots):
        branch = slot_branch[(rank * lax.axis_size("prompt") + mine) * slots + s]
        lengths.append(branch_length[branch])
        owners.append(branch_prompt[branch])

    for name in LAST_LOADS:
        load(name).wait()

    for g in range(slots):
        for c in range(spans):
            gates(g, c)

    quanta = 2 * slots * spans * packs
    early = jnp.where(rank == 0, quanta, jnp.minimum(EARLY * (rank - 1), quanta))
    lax.fori_loop(0, early, lambda w, x: (quantum(w), x)[1], 0)
    back_lag = BACK * (last - rank)
    apply_lag = back_lag + AFTER

    def tick(t, carry):
        pl.when(t < heads)(lambda: step_forward(t))
        j = t - back_lag
        pl.when((j >= 0) & (j < heads))(lambda: step_back(j))
        w = t + early
        pl.when(w < quanta)(lambda: quantum(w))
        a = t - apply_lag

        @pl.when((a >= 0) & (a < heads) & (a % REP == REP - 1))
        def _():
            for r in range(REP):
                across(other, a - r).wait_recv()
            step_apply(a // REP)

        return carry

    lax.fori_loop(0, jnp.maximum(heads + apply_lag, quanta - early), tick, 0)

    def finish(i, carry):
        @pl.when(rank < last)
        def _():
            forward(i).wait_send()

        @pl.when(rank > 0)
        def _():
            backward(i).wait_send()


        across(mine, i).wait_send()
        return carry

    lax.fori_loop(0, heads, finish, 0)


LOADED = (
    "pq", "pk", "pv", "pbeta", "pdecay", "sq", "sk", "sv", "sbeta", "sdecay",
    "gain", "masks", "cum", "pick",
)
FIRST_LOADS = ("pdecay", "pbeta", "cum", "masks", "pk", "pq", "pick", "pv", "gain")
LAST_LOADS = ("sdecay", "sbeta", "sk", "sq", "sv")
LOAD_ORDER = FIRST_LOADS + LAST_LOADS
BACK = 5
AFTER = 2
EARLY = 3
FIRST = 8
PACK = 8


def settle_kernel(count, *refs):
    copies = [
        pltpu.make_async_copy(a, b, refs[2 * count].at[n])
        for n, (a, b) in enumerate(zip(refs[:count], refs[count : 2 * count]))
    ]
    for c in copies:
        c.start()
    for c in copies:
        c.wait()


def settle(*arrays):
    count = len(arrays)
    return pl.pallas_call(
        functools.partial(settle_kernel, count),
        out_shape=[jax.ShapeDtypeStruct(x.shape, x.dtype) for x in arrays],
        in_specs=[pl.BlockSpec(memory_space=pltpu.VMEM)] * count,
        out_specs=[pl.BlockSpec(memory_space=pl.ANY)] * count,
        scratch_shapes=[pltpu.SemaphoreType.DMA((count,))],
        compiler_params=pltpu.CompilerParams(vmem_limit_bytes=8 * 1024 * 1024),
        name="settle",
    )(*arrays)


def local(
    prompt_queries, prompt_keys, prompt_values, prompt_beta, prompt_decay,
    suffix_queries, suffix_keys, suffix_values, suffix_beta, suffix_decay,
    norm_gain, slot_branch, branch_length, branch_prompt,
):
    key_heads = prompt_queries.shape[2] // DK
    heads = key_heads * REP
    slots, spans = suffix_queries.shape[0], suffix_queries.shape[1] // CH
    space = pl.BlockSpec(memory_space=pl.ANY)
    pack = PACK if key_heads % PACK == 0 else key_heads
    state = pltpu.VMEM((heads, DK, DV), F32)
    loads = (
        prompt_queries, prompt_keys, prompt_values, prompt_beta, prompt_decay,
        suffix_queries, suffix_keys, suffix_values, suffix_beta, suffix_decay,
        norm_gain[None, :], *(jnp.asarray(x) for x in tables()),
    )
    outs = pl.pallas_call(
        chain_kernel,
        out_shape=[
            pltpu.VMEM(prompt_values.shape, BF16),
            pltpu.VMEM(suffix_values.shape, BF16),
        ],
        in_specs=[space] * len(loads) + [space] * 3,
        out_specs=[pl.BlockSpec(memory_space=pltpu.VMEM)] * 2,
        scratch_shapes=[pltpu.VMEM(x.shape, x.dtype) for x in loads]
        + [
            pltpu.VMEM((heads, 2 * CH, DK), BF16),
            state,
            pltpu.VMEM((heads, 8, DV), F32),
            state,
            state,
            pltpu.VMEM((2, heads, DK, DV), F32),
            pltpu.VMEM((slots, spans, heads, CH, 2 * CH), BF16),
            pltpu.VMEM((slots, spans, key_heads, CH, 2 * CH), BF16),
            pltpu.VMEM((slots, spans, key_heads, CH, DK), BF16),
            pltpu.VMEM((slots, spans, key_heads, CH, REP), F32),
            pltpu.VMEM((slots, spans, heads, 8, DV), F32),
            pltpu.VMEM((slots, spans, heads, SB, CH), F32),
            pltpu.VMEM((slots, spans, heads, 8, CH), F32),
            pltpu.VMEM((pack, CH, 2 * CH), BF16),
            pltpu.VMEM((pack, 2 * SB, CH), BF16),
            *(pltpu.SMEM(x.shape, x.dtype) for x in (slot_branch, branch_length, branch_prompt)),
            pltpu.SemaphoreType.DMA((len(loads),)),
            pltpu.SemaphoreType.DMA((3,)),
        ]
        + [pltpu.SemaphoreType.DMA((heads,))] * 6,
        compiler_params=pltpu.CompilerParams(
            collective_id=0, has_side_effects=True, vmem_limit_bytes=60 * 1024 * 1024
        ),
        name="chain",
    )(*loads, slot_branch, branch_length, branch_prompt)
    return tuple(settle(*outs))


def solution(mesh):
    lead = P(("groups", "prompt"), "seq", "head")
    lead_gate = P(("groups", "prompt"), "head", "seq")
    slot = P(("groups", "seq", "prompt"), None, "head")
    slot_gate = P(("groups", "seq", "prompt"), "head", None)
    return jax.shard_map(
        local,
        mesh=mesh,
        in_specs=(
            lead, lead, lead, lead_gate, lead_gate, slot, slot, slot, slot_gate, slot_gate,
            P(), P("groups"), P("groups"), P("groups"),
        ),
        out_specs=(lead, slot),
        check_vma=False,
    )
```

```python
import functools

import jax
import jax.numpy as jnp
import ml_dtypes
import numpy as np
from jax import lax
from jax.experimental import pallas as pl
from jax.experimental.pallas import tpu as pltpu
from jax.sharding import PartitionSpec as P

DK = 128
DV = 128
CH = 128
SB = 16
REP = 2
EPS_NORM = 1e-06
F32 = jnp.float32
BF16 = jnp.bfloat16
MESH = pl.DeviceIdType.MESH
NN = (((1,), (0,)), ((), ()))
NT = (((1,), (1,)), ((), ()))
TN = (((0,), (0,)), ((), ()))

BD = {16: 0, 32: 2, 64: 4}
SWAP = {16: 1, 32: 3, 64: 5}
UPTO, BACKWARDS, THIN = 6, 7, 8
EVEN = {16: 0, 32: 32, 64: 64}
ODD = {16: 16, 32: 48, 64: 80}
STRICT, EYE = 96, 112


def tables():
    l = np.arange(CH)
    r, c = l[:, None], l[None]
    i = np.arange(SB)[:, None]
    squares = []
    for s in (16, 32, 64):
        squares += [r // s == c // s, (r // s) ^ 1 == c // s]
    thin = []
    for s in (16, 32, 64):
        thin += [np.broadcast_to((c // s) % 2 == p, (SB, CH)) for p in (0, 1)]
    thin += [i > c % SB, i == c % SB]
    squares += [r >= c, r ^ (CH - SB) == c, np.concatenate(thin, 0)]
    cum = np.concatenate([r <= c, r <= (c ^ (CH - SB))], 1)
    pick = np.concatenate([r == (c // SB) * SB + k for k in range(SB)], 1)
    b = lambda x: x.astype(np.float32).astype(ml_dtypes.bfloat16)
    return b(np.stack(squares)), b(cum), b(pick)


def mm(a, b, dims=NN):
    return lax.dot_general(a, b, dims, preferred_element_type=F32)


def unit(x):
    w = x.astype(F32)
    return (w * lax.rsqrt(jnp.sum(w * w, axis=-1, keepdims=True) + EPS_NORM)).astype(BF16)


def flip(x):
    return jnp.concatenate([x[i : i + SB] for i in range(CH - SB, -1, -SB)], axis=0)


def tile(x, n):
    return x if n == 1 else jnp.concatenate([x] * n, axis=0)


def terms(x, n):
    parts = []
    for _ in range(n):
        p = x.astype(BF16)
        parts.append(p)
        x = x - p.astype(F32)
    return jnp.concatenate(parts, axis=1)


def running_log(decay, cum):
    both = mm(terms(decay, 3), tile(cum[...], 3))
    return both[:, :CH], both[:, CH:]


def spread_beta(beta, masks):
    eye = masks[THIN, EYE:].astype(F32)
    rows = jnp.concatenate([beta[h : h + 1] * eye for h in range(beta.shape[0])], axis=0)
    return mm(terms(rows, 2), tile(masks[BD[16]], 2))


def small_inverses(grams, betas, masks, pick):
    n = len(grams)
    blocks = CH // SB
    thin = lambda at: masks[THIN, at : at + SB]
    strict = thin(STRICT)
    compact = []
    for g in grams:
        c = g[:SB, :CH] * masks[BD[16], :SB]
        for b in range(1, blocks):
            c = c + g[b * SB : (b + 1) * SB, :CH] * masks[BD[16], b * SB : (b + 1) * SB]
        compact.append(c * strict)
    flat = jnp.concatenate(compact, axis=0)
    eye = thin(EYE).astype(F32)
    top = [-eye[:8]] * (n * REP)
    low = [-eye[8:]] * (n * REP)
    for k in range(SB - 1):
        if k % 2 == 0:
            pair = mm(flat, pick[:, k * CH : (k + 2) * CH])
        e = pair[:, (k % 2) * CH : (k % 2 + 1) * CH]
        for j in range(n):
            for r in range(REP):
                h = j * REP + r
                row = (top[h][k : k + 1] if k < 8 else low[h][k - 8 : k - 7]) * betas[h][k : k + 1]
                if k < 7:
                    top[h] = top[h] - e[j * SB : j * SB + 8] * row
                low[h] = low[h] - e[j * SB + 8 : (j + 1) * SB] * row
    done = [
        (jnp.concatenate([top[h], low[h]], axis=0) * betas[h]).astype(BF16) for h in range(n * REP)
    ]
    first = done[0::2]
    second = mm(jnp.concatenate(done[1::2], axis=0), masks[BACKWARDS]).astype(BF16)
    second = [second[j * SB : (j + 1) * SB] for j in range(n)]
    return first, second


def merge(grams, first, second, masks):
    thin = lambda at: masks[THIN, at : at + SB]
    size = SB
    while size < CH:
        rows = size // SB
        even, odd = tile(thin(EVEN[size]), rows), tile(thin(ODD[size]), rows)
        cross = []
        for g in grams:
            parts = []
            for i in range(rows):
                part = None
                for p in range(CH // (2 * size)):
                    at = (2 * p + 1) * size + i * SB
                    ahead = masks[BD[size], 2 * p * size : 2 * p * size + SB]
                    behind = masks[BD[size], (2 * p + 1) * size : (2 * p + 1) * size + SB]
                    back = CH - SB - (2 * p * size + i * SB)
                    term = g[at : at + SB, :CH] * ahead + g[back : back + SB, CH:] * behind
                    part = term if part is None else part + term
                parts.append(part)
            cross.append(jnp.concatenate(parts, axis=0))
        reps = CH // size
        split = [(a * even, a * odd, b * even, b * odd) for a, b in zip(first, second)]
        mids = [
            mm(c, tile(ae + bo, reps) * masks[BD[size]]).astype(BF16)
            for c, (ae, ao, be, bo) in zip(cross, split)
        ]
        offs = [
            mm(ao + be, tile(m, reps) * masks[SWAP[size]]).astype(BF16)
            for m, (ae, ao, be, bo) in zip(mids, split)
        ]
        first = [
            jnp.concatenate([ae, o * even + ao], axis=0) for o, (ae, ao, be, bo) in zip(offs, split)
        ]
        second = [
            jnp.concatenate([be + o * odd, bo], axis=0) for o, (ae, ao, be, bo) in zip(offs, split)
        ]
        size *= 2
    return first, [flip(x) for x in second]


def grams_of(queries, keys, masks):
    qs, ks = [unit(q) for q in queries], [unit(k) for k in keys]
    backs = [flip(k) for k in ks]
    looks = [mm(q, k, NT).astype(BF16) * masks[UPTO] for q, k in zip(qs, ks)]
    grams = [mm(k, jnp.concatenate([k, b], axis=0), NT).astype(BF16) for k, b in zip(ks, backs)]
    return qs, ks, backs, looks, grams


def norm_rows(o, gain):
    return o * lax.rsqrt(jnp.mean(o * o, axis=-1, keepdims=True) + EPS_NORM) * gain


def chain_kernel(
    *refs,
):
    count = len(LOADED)
    given, facts, (pout, sout) = refs[:count], refs[count : count + 3], refs[count + 3 : count + 5]
    held, rest = refs[count + 5 : 2 * count + 5], refs[2 * count + 5 :]
    pq, pk, pv, pbeta, pdecay, sq, sk, sv, sbeta, sdecay, gain_ref, masks, cum, pick = held
    (
        step_ref, seen_ref, fade_ref, inbox, outbox, finals,
        s_left, s_look, s_key, s_eps, s_end, g_beta, g_grow, w_gram, w_small,
        *told, load_sem, fact_sem,
        fsend, frecv, bsend, brecv, csend, crecv,
    ) = rest
    slot_branch, branch_length, branch_prompt = told
    key_heads = pq.shape[2] // DK
    heads = key_heads * REP
    slots, spans = sq.shape[0], sq.shape[1] // CH
    pack = PACK if key_heads % PACK == 0 else key_heads
    packs = key_heads // pack
    rank, last = lax.axis_index("seq"), lax.axis_size("seq") - 1
    mine = lax.axis_index("prompt")
    other = 1 - mine

    def load(name):
        n = LOADED.index(name)
        return pltpu.make_async_copy(given[n], held[n], load_sem.at[n])

    for name in LOAD_ORDER:
        load(name).start()
    tell = [
        pltpu.make_async_copy(a, b, fact_sem.at[n]) for n, (a, b) in enumerate(zip(facts, told))
    ]
    for c in tell:
        c.start()

    def forward(i):
        return pltpu.make_async_remote_copy(
            src_ref=outbox.at[i], dst_ref=inbox.at[i], send_sem=fsend.at[i],
            recv_sem=frecv.at[i], device_id={"seq": rank + 1}, device_id_type=MESH,
        )

    def backward(i):
        return pltpu.make_async_remote_copy(
            src_ref=finals.at[mine, i], dst_ref=finals.at[mine, i], send_sem=bsend.at[i],
            recv_sem=brecv.at[i], device_id={"seq": rank - 1}, device_id_type=MESH,
        )

    def across(p, i):
        return pltpu.make_async_remote_copy(
            src_ref=finals.at[p, i], dst_ref=finals.at[p, i], send_sem=csend.at[i],
            recv_sem=crecv.at[i], device_id={"prompt": other}, device_id_type=MESH,
        )

    barrier = pltpu.get_barrier_semaphore()

    def greet(where):
        pl.semaphore_signal(barrier, inc=1, device_id=where, device_id_type=MESH)

    greet({"prompt": other})

    @pl.when(rank > 0)
    def _():
        greet({"seq": rank - 1})

    @pl.when(rank < last)
    def _():
        greet({"seq": rank + 1})


    def meet():
        pl.semaphore_wait(barrier, 1 + jnp.where(rank > 0, 1, 0) + jnp.where(rank < last, 1, 0))

    for name in FIRST_LOADS:
        load(name).wait()

    def prepare(g, size):
        cols = [slice(j * DK, (j + 1) * DK) for j in range(g, g + size)]
        hs = slice(g * REP, (g + size) * REP)
        log_row, log_back = running_log(pdecay[0, hs], cum)
        beta = spread_beta(pbeta[0, hs], masks)
        betas = [beta[h * SB : (h + 1) * SB] for h in range(size * REP)]
        mid = log_row[:, CH // 2 - 1 : CH // 2]
        end = log_row[:, CH - 1 :]
        grow = (-jnp.exp(mid - log_row), -jnp.exp(mid - log_back))
        from_mid = jnp.exp(end - mid)
        qs, ks, backs, looks, grams = grams_of(
            [pq[0, :, c] for c in cols], [pk[0, :, c] for c in cols], masks
        )
        first, second = merge(grams, *small_inverses(grams, betas, masks, pick), masks)
        rights = []
        for j in range(size):
            right = []
            for r, left in enumerate((first[j], second[j])):
                h = j * REP + r
                v = pv[0, :, (hs.start + h) * DV : (hs.start + h + 1) * DV]
                scaled = (left.astype(F32) * grow[r][h : h + 1]).astype(BF16)
                right.append(mm(scaled, flip(v) if r else v).astype(BF16))
            rights.append(jnp.concatenate(right, axis=1))
            writes = mm(ks[j], rights[j], TN)
            for r in range(REP):
                h = j * REP + r
                outbox[hs.start + h] = from_mid[h : h + 1] * writes[:, r * DV : (r + 1) * DV]

        def rest():
            shrink = jnp.exp(log_row - mid).T
            at_mid, at_end = jnp.exp(mid), jnp.exp(end)
            for j in range(size):
                turn = jnp.concatenate(
                    [mm(first[j], ks[j]).astype(BF16), mm(second[j], backs[j]).astype(BF16)], axis=1
                )
                moves = mm(ks[j], turn, TN)
                reads = mm(looks[j], jnp.concatenate([turn, rights[j]], axis=1))
                for r in range(REP):
                    h = j * REP + r
                    cut, off = slice(r * DV, (r + 1) * DV), slice((REP + r) * DV, (REP + r + 1) * DV)
                    rows = jnp.broadcast_to(shrink[:, h : h + 1], (CH, DV))
                    step_ref[hs.start + h] = jnp.concatenate(
                        [
                            (at_end[h : h + 1] * moves[:, cut]).astype(BF16),
                            (
                                rows * (at_mid[h : h + 1] * (qs[j].astype(F32) + reads[:, cut]))
                            ).astype(BF16),
                        ],
                        axis=0,
                    )
                    seen_ref[hs.start + h] = rows * reads[:, off]
                    fade_ref[hs.start + h] = jnp.broadcast_to(at_end[h : h + 1], (8, DV))

        return rest

    def show(h, o):
        at = pl.ds(pl.multiple_of(h * DV, DV), DV)
        pout[0, :, at] = norm_rows(o, gain_ref[...]).astype(BF16)

    def step_forward(i):
        @pl.when(rank == 0)
        def _():
            show(i, seen_ref[i])

        @pl.when(rank > 0)
        def _():
            forward(i).wait_recv()
            state = inbox[i]
            both = mm(step_ref[i], state.astype(BF16))
            grown = fade_ref[i, :1] * state + both[:DK] + outbox[i]

            @pl.when(rank < last)
            def _():
                outbox[i] = grown
                forward(i).start()

            @pl.when(rank == last)
            def _():
                finals[mine, i] = grown
                across(mine, i).start()
                backward(i).start()

            show(i, both[DK:] + seen_ref[i])

    def step_back(i):
        @pl.when(rank < last)
        def _():
            backward(i).wait_recv()

            @pl.when(rank > 0)
            def _():
                backward(i).start()

            across(mine, i).start()

    def gates(s, c):
        span = slice(c * CH, (c + 1) * CH)
        log_row, log_back = running_log(sdecay[s, :, span], cum)
        beta = spread_beta(sbeta[s, :, span], masks)
        grow = (-jnp.exp(-log_row), -jnp.exp(-log_back))
        eps = (EPS_NORM * jnp.exp(-2.0 * log_row)).T
        end = jnp.exp(log_row[:, CH - 1 :])
        for h in range(heads):
            g_beta[s, c, h] = beta[h * SB : (h + 1) * SB]
            g_grow[s, c, h] = jnp.broadcast_to(grow[h % REP][h : h + 1], (8, CH))
            s_end[s, c, h] = jnp.broadcast_to(end[h : h + 1], (8, DV))
        for j in range(key_heads):
            s_eps[s, c, j] = eps[:, j * REP : (j + 1) * REP]

    def where_of(m):
        g, place = m // (slots * spans), m % (slots * spans)
        return place // spans, place % spans, g

    def work_grams(m):
        s, c, g = where_of(m)
        rows = pl.ds(pl.multiple_of(c * CH, CH), CH)
        at = pl.ds(pl.multiple_of(g * pack * DK, pack * DK), pack * DK)
        q, k = sq[s, rows, at], sk[s, rows, at]
        qs, ks, backs, looks, grams = grams_of(
            [q[:, j * DK : (j + 1) * DK] for j in range(pack)],
            [k[:, j * DK : (j + 1) * DK] for j in range(pack)],
            masks,
        )
        betas = [g_beta[s, c, g * pack * REP + h] for h in range(pack * REP)]
        first, second = small_inverses(grams, betas, masks, pick)
        for j in range(pack):
            to = g * pack + j
            s_key[s, c, to] = ks[j]
            s_look[s, c, to] = jnp.concatenate([qs[j], looks[j]], axis=1)
            w_gram[j] = grams[j]
            w_small[j] = jnp.concatenate([first[j], second[j]], axis=0)

    def work_merge(m):
        s, c, g = where_of(m)
        first, second = merge(
            [w_gram[j] for j in range(pack)],
            [w_small[j, :SB] for j in range(pack)],
            [w_small[j, SB:] for j in range(pack)],
            masks,
        )
        for j in range(pack):
            for r, left in enumerate((first[j], second[j])):
                h = (g * pack + j) * REP + r
                scaled = (left.astype(F32) * g_grow[s, c, h, :1]).astype(BF16)
                s_left[s, c, h] = jnp.concatenate([scaled, left], axis=1)

    def quantum(w):
        pl.when(w % 2 == 0)(lambda: work_grams(w // 2))
        pl.when(w % 2 == 1)(lambda: work_merge(w // 2))

    def step_apply(j):
        at = pl.ds(pl.multiple_of(j * REP * DV, REP * DV), REP * DV)
        place = lax.broadcasted_iota(jnp.int32, (CH, 1), 0)
        gain = gain_ref[...]
        states = [
            [
                jnp.where(owners[s] == 0, finals[0, j * REP + r], finals[1, j * REP + r])
                for r in range(REP)
            ]
            for s in range(slots)
        ]
        for c in range(spans):
            span = slice(c * CH, (c + 1) * CH)
            narrow = [
                jnp.concatenate([x.astype(BF16) for x in states[s]], axis=1) for s in range(slots)
            ]
            reads = [mm(s_key[s, c, j], narrow[s]).astype(BF16) for s in range(slots)]
            news = []
            for s in range(slots):
                v = sv[s, span, at]
                pair = []
                for r in range(REP):
                    cut = slice(r * DV, (r + 1) * DV)
                    a, b = v[:, cut], reads[s][:, cut]
                    if r:
                        a, b = flip(a), flip(b)
                    pair.append(
                        mm(s_left[s, c, j * REP + r], jnp.concatenate([a, b], axis=0)).astype(BF16)
                    )
                news.append(jnp.concatenate(pair, axis=1))
            if c + 1 < spans:
                for s in range(slots):
                    added = mm(s_key[s, c, j], news[s], TN)
                    states[s] = [
                        s_end[s, c, j * REP + r, :1]
                        * (states[s][r] + added[:, r * DV : (r + 1) * DV])
                        for r in range(REP)
                    ]
            for s in range(slots):
                o = mm(s_look[s, c, j], jnp.concatenate([narrow[s], news[s]], axis=0))
                live = place + c * CH < lengths[s]
                normed = []
                for r in range(REP):
                    x = o[:, r * DV : (r + 1) * DV]
                    eps = s_eps[s, c, j, :, r : r + 1]
                    scale = lax.rsqrt(jnp.mean(x * x, axis=-1, keepdims=True) + eps)
                    normed.append((x * jnp.where(live, scale, 0.0) * gain).astype(BF16))
                sout[s, span, at] = jnp.concatenate(normed, axis=1)

    size = FIRST if key_heads % FIRST == 0 else key_heads
    later = []
    for g in range(0, key_heads, size):
        later.append(prepare(g, size))
        if g == 0:
            meet()

        @pl.when(rank == 0)
        def _():
            for h in range(g * REP, (g + size) * REP):
                forward(h).start()

    for rest in later:
        rest()

    for c in tell:
        c.wait()
    lengths, owners = [], []
    for s in range(slots):
        branch = slot_branch[(rank * lax.axis_size("prompt") + mine) * slots + s]
        lengths.append(branch_length[branch])
        owners.append(branch_prompt[branch])

    for name in LAST_LOADS:
        load(name).wait()

    for g in range(slots):
        for c in range(spans):
            gates(g, c)

    quanta = 2 * slots * spans * packs
    early = jnp.where(rank == 0, quanta, jnp.minimum(EARLY * (rank - 1), quanta))
    lax.fori_loop(0, early, lambda w, x: (quantum(w), x)[1], 0)
    back_lag = BACK * (last - rank)
    apply_lag = back_lag + AFTER

    def tick(t, carry):
        pl.when(t < heads)(lambda: step_forward(t))
        j = t - back_lag
        pl.when((j >= 0) & (j < heads))(lambda: step_back(j))
        w = t + early
        pl.when(w < quanta)(lambda: quantum(w))
        a = t - apply_lag

        @pl.when((a >= 0) & (a < heads) & (a % REP == REP - 1))
        def _():
            for r in range(REP):
                across(other, a - r).wait_recv()
            step_apply(a // REP)

        return carry

    lax.fori_loop(0, jnp.maximum(heads + apply_lag, quanta - early), tick, 0)

    def finish(i, carry):
        @pl.when(rank < last)
        def _():
            forward(i).wait_send()

        @pl.when(rank > 0)
        def _():
            backward(i).wait_send()


        across(mine, i).wait_send()
        return carry

    lax.fori_loop(0, heads, finish, 0)


LOADED = (
    "pq", "pk", "pv", "pbeta", "pdecay", "sq", "sk", "sv", "sbeta", "sdecay",
    "gain", "masks", "cum", "pick",
)
FIRST_LOADS = ("pdecay", "pbeta", "cum", "masks", "pk", "pq", "pick", "pv", "gain")
LAST_LOADS = ("sdecay", "sbeta", "sk", "sq", "sv")
LOAD_ORDER = FIRST_LOADS + LAST_LOADS
BACK = 5
AFTER = 2
EARLY = 3
PIECES = 2
FIRST = 8
PACK = 8


def settle_kernel(count, *refs):
    copies = []
    for a, b in zip(refs[:count], refs[count : 2 * count]):
        rows = a.shape[1] // PIECES
        for s in range(a.shape[0]):
            for p in range(PIECES):
                cut = (s, pl.ds(p * rows, rows))
                sem = refs[2 * count].at[len(copies)]
                copies.append(pltpu.make_async_copy(a.at[cut], b.at[cut], sem))
    for c in copies:
        c.start()
    for c in copies:
        c.wait()


def settle(*arrays):
    count = len(arrays)
    return pl.pallas_call(
        functools.partial(settle_kernel, count),
        out_shape=[jax.ShapeDtypeStruct(x.shape, x.dtype) for x in arrays],
        in_specs=[pl.BlockSpec(memory_space=pltpu.VMEM)] * count,
        out_specs=[pl.BlockSpec(memory_space=pl.ANY)] * count,
        scratch_shapes=[pltpu.SemaphoreType.DMA((sum(x.shape[0] for x in arrays) * PIECES,))],
        compiler_params=pltpu.CompilerParams(vmem_limit_bytes=8 * 1024 * 1024),
        name="settle",
    )(*arrays)


def local(
    prompt_queries, prompt_keys, prompt_values, prompt_beta, prompt_decay,
    suffix_queries, suffix_keys, suffix_values, suffix_beta, suffix_decay,
    norm_gain, slot_branch, branch_length, branch_prompt,
):
    key_heads = prompt_queries.shape[2] // DK
    heads = key_heads * REP
    slots, spans = suffix_queries.shape[0], suffix_queries.shape[1] // CH
    space = pl.BlockSpec(memory_space=pl.ANY)
    pack = PACK if key_heads % PACK == 0 else key_heads
    state = pltpu.VMEM((heads, DK, DV), F32)
    loads = (
        prompt_queries, prompt_keys, prompt_values, prompt_beta, prompt_decay,
        suffix_queries, suffix_keys, suffix_values, suffix_beta, suffix_decay,
        norm_gain[None, :], *(jnp.asarray(x) for x in tables()),
    )
    outs = pl.pallas_call(
        chain_kernel,
        out_shape=[
            pltpu.VMEM(prompt_values.shape, BF16),
            pltpu.VMEM(suffix_values.shape, BF16),
        ],
        in_specs=[space] * len(loads) + [space] * 3,
        out_specs=[pl.BlockSpec(memory_space=pltpu.VMEM)] * 2,
        scratch_shapes=[pltpu.VMEM(x.shape, x.dtype) for x in loads]
        + [
            pltpu.VMEM((heads, 2 * CH, DK), BF16),
            state,
            pltpu.VMEM((heads, 8, DV), F32),
            state,
            state,
            pltpu.VMEM((2, heads, DK, DV), F32),
            pltpu.VMEM((slots, spans, heads, CH, 2 * CH), BF16),
            pltpu.VMEM((slots, spans, key_heads, CH, 2 * CH), BF16),
            pltpu.VMEM((slots, spans, key_heads, CH, DK), BF16),
            pltpu.VMEM((slots, spans, key_heads, CH, REP), F32),
            pltpu.VMEM((slots, spans, heads, 8, DV), F32),
            pltpu.VMEM((slots, spans, heads, SB, CH), F32),
            pltpu.VMEM((slots, spans, heads, 8, CH), F32),
            pltpu.VMEM((pack, CH, 2 * CH), BF16),
            pltpu.VMEM((pack, 2 * SB, CH), BF16),
            *(pltpu.SMEM(x.shape, x.dtype) for x in (slot_branch, branch_length, branch_prompt)),
            pltpu.SemaphoreType.DMA((len(loads),)),
            pltpu.SemaphoreType.DMA((3,)),
        ]
        + [pltpu.SemaphoreType.DMA((heads,))] * 6,
        compiler_params=pltpu.CompilerParams(
            collective_id=0, has_side_effects=True, vmem_limit_bytes=60 * 1024 * 1024
        ),
        name="chain",
    )(*loads, slot_branch, branch_length, branch_prompt)
    return tuple(settle(*outs))


def solution(mesh):
    lead = P(("groups", "prompt"), "seq", "head")
    lead_gate = P(("groups", "prompt"), "head", "seq")
    slot = P(("groups", "seq", "prompt"), None, "head")
    slot_gate = P(("groups", "seq", "prompt"), "head", None)
    return jax.shard_map(
        local,
        mesh=mesh,
        in_specs=(
            lead, lead, lead, lead_gate, lead_gate, slot, slot, slot, slot_gate, slot_gate,
            P(), P("groups"), P("groups"), P("groups"),
        ),
        out_specs=(lead, slot),
        check_vma=False,
    )
```
